256 devices in a mesh: gx: 8 (over z), gy: 4 (over y_lo, core), gz: 8 (over y_hi, x).
Axes of the slice: x: 4, y: 4 (y_hi: 2, y_lo: 2; y = y_hi * 2 + y_lo), z: 8, core: 2. Of those that a mesh axis runs over, the one named last changes fastest.
Arguments:
- state: bfloat16 [128, 64, 16, 8, 128], P('gx', 'gy', 'gz'), may hold values from -6 to 6
- cotangent: bfloat16 [128, 64, 16, 8, 128], P('gx', 'gy', 'gz'), may hold values from -6 to 6
- counts: int32 [8], P('gz'), may hold values from 1 to 2, 12 in all
- edge_weights: bfloat16 [2, 2, 128, 128], replicated, may hold values from -0.5 to 0.5
- node_in: bfloat16 [2, 256, 128], replicated, may hold values from -0.375 to 0.375
- node_out: bfloat16 [2, 128, 128], replicated, may hold values from -0.5 to 0.5
- biases: float32 [2, 2, 128], replicated, may hold values from -4 to 4
Outputs:
- state_grad: bfloat16 [128, 64, 16, 8, 128], P('gx', 'gy', 'gz')
- edge_grads: float32 [2, 2, 128, 128], replicated
- node_in_grad: float32 [2, 256, 128], replicated
- node_out_grad: float32 [2, 128, 128], replicated
- bias_grads: float32 [2, 2, 128], replicated
The draws below stay inside these ranges and needn't reach their ends.
Inputs may be any that keep to these rules, and one draw needn't show every extreme that they name: The counts sum to 12; index k of gz holds the element layers that follow those of smaller indices.
All inputs are finite; a program needn't handle non-finite values. No bound on the sum of `counts` on one device may be relied on, other than what follows from the above.
Results may differ from the reference program's by a relative error of at most 0.012.
The reference program's roundings to bfloat16 on the way count: a program that leaves them out, or rounds other values in their place, can miss the bound.
Values sent between devices are 32-bit elements; how exact they have to be, the bound alone decides.
A program may use at most 128 MiB of HBM per device.

```python
import math
import jax
import jax.numpy as jnp
import numpy as np
from jax import lax

H = 128
NODE = 8
EB = 2
LZ = 2
LAYERS_ALL = 12
NODES_ALL = 786432
N_GX = 8
N_GY = 4
N_GZ = 8


def block_levels(rng, extent, pieces, least, largest):
    def one(axis_at, parts):
        draws = jax.random.uniform(jax.random.fold_in(jax.random.fold_in(rng, 6), axis_at), (parts,), jnp.float32, least / len(pieces), largest / len(pieces))
        return jnp.repeat(jnp.exp(draws), extent[axis_at] // parts).reshape((-1,) + (1,) * (len(extent) - axis_at - 1))

    gain = one(*pieces[0])
    for cut in pieces[1:]:
        gain = gain * one(*cut)
    return gain


def length_profile(amount, total, limit, slope):
    loads = [(1 << 20) // math.isqrt(standing ** slope) + 1 for standing in range(2, amount + 1)]
    rest, given = total - limit - (amount - 1), [1] * (amount - 1)
    while rest > 0:
        free = [i for i in range(amount - 1) if given[i] < limit]
        mass, remaining = sum([loads[i] for i in free]), rest
        for i in free:
            addition = min(limit - given[i], max(1, remaining * loads[i] // mass), rest)
            given[i] = given[i] + addition
            rest = rest - addition
    return np.array([limit] + given)


def ragged_sizes(stream_key, count, total, limit, skew):
    if count == 2:
        one = jax.random.randint(stream_key, (), max(1, total - limit), min(limit, total - 1) + 1)
        return jnp.stack([one, total - one])
    sizes = jnp.asarray(length_profile(count, total, limit, skew), jnp.int32)
    pairs = (count - 1) // 2
    giver, sink = sizes[1:1 + 2 * pairs:2], sizes[2:2 + 2 * pairs:2]
    margin = jnp.minimum(giver - 1, limit - sink)
    moved = jax.random.randint(jax.random.fold_in(stream_key, 1), (pairs,), 0, 1 << 20) % (margin + 1)
    sizes = sizes.at[1:1 + 2 * pairs:2].set(giver - moved).at[2:2 + 2 * pairs:2].set(sink + moved)
    return sizes[jax.random.permutation(jax.random.fold_in(stream_key, 2), count)]


def gaussian(rng, shape, width, bound, cuts=(), kind=jnp.bfloat16):
    values = width * jax.random.normal(rng, shape, jnp.float32)
    if cuts:
        values = values * block_levels(rng, shape, cuts, -0.22, 0.18)
    return jnp.clip(values, -bound, bound).astype(kind)


def setup_inputs(seed: int = 0) -> dict:
    arg_keys = jax.random.split(jax.random.key(seed), 8)
    return {
        "state": gaussian(arg_keys[0], (NODE * EB * N_GX, NODE * EB * N_GY, LZ * N_GZ, NODE, H), 1.0, 6.0, ((0, 8), (1, 4), (2, 8))),
        "cotangent": gaussian(arg_keys[1], (NODE * EB * N_GX, NODE * EB * N_GY, LZ * N_GZ, NODE, H), 1.0, 6.0, ((0, 8), (1, 4), (2, 8))),
        "counts": ragged_sizes(arg_keys[2], N_GZ, LAYERS_ALL, LZ, 2).astype(jnp.int32),
        "edge_weights": gaussian(arg_keys[3], (2, 2, H, H), H ** -0.5, 0.5),
        "node_in": gaussian(arg_keys[4], (2, 2 * H, H), (2 * H) ** -0.5, 0.375),
        "node_out": gaussian(arg_keys[5], (2, H, H), H ** -0.5, 0.5),
        "biases": gaussian(arg_keys[6], (2, 2, H), 1.0, 4.0, (), jnp.float32),
    }


edge_dims = (1, 3, 5)

def slice_along(array, start, stop, dim_no):
    return lax.slice_in_dim(array, start, stop, axis=dim_no)

def matmul_rows(left, weight):
    flattened = left.reshape(-1, left.shape[-1])
    product = jnp.dot(flattened, weight, preferred_element_type=jnp.float32)
    return product.reshape(left.shape[:-1] + (weight.shape[-1],))

def cross_rows(left, right):
    return lax.dot_general(left.reshape(-1, left.shape[-1]), right.reshape(-1, right.shape[-1]), (((0,), (0,)), ((), ())), preferred_element_type=jnp.float32)

def spread_diff(values, dim_no):
    zero_row = jnp.zeros_like(slice_along(values, 0, 1, dim_no))
    return jnp.concatenate([zero_row, values], dim_no) - jnp.concatenate([values, zero_row], dim_no)

def silu_slope(values):
    sig_value = jax.nn.sigmoid(values)
    return sig_value * (1.0 + values * (1.0 - sig_value))

def edges_forward(features, weight_one, weight_two, bias_edge):
    widened = features.astype(jnp.float32)
    messages = jnp.zeros(features.shape, jnp.float32)
    stored = []
    for dim_no in edge_dims:
        length = features.shape[dim_no]
        differ = (slice_along(widened, 1, length, dim_no) - slice_along(widened, 0, length - 1, dim_no)).astype(jnp.bfloat16)
        before = matmul_rows(differ, weight_one) + bias_edge
        active = jax.nn.silu(before).astype(jnp.bfloat16)
        messages = messages + spread_diff(matmul_rows(active, weight_two), dim_no)
        stored.append((differ, before, active))
    return (messages, stored)

def edges_backward(grad_msg, stored, weight_one, weight_two):
    feat_width = grad_msg.shape[-1]
    grad_feat = jnp.zeros(grad_msg.shape, jnp.float32)
    grad_one = jnp.zeros((feat_width, feat_width), jnp.float32)
    grad_two = jnp.zeros((feat_width, feat_width), jnp.float32)
    grad_bias = jnp.zeros((feat_width,), jnp.float32)
    for dim_no, entry in zip(edge_dims, stored):
        differ, before, active = entry
        length = grad_msg.shape[dim_no]
        grad_out = (slice_along(grad_msg, 1, length, dim_no) - slice_along(grad_msg, 0, length - 1, dim_no)).astype(jnp.bfloat16)
        grad_two = grad_two + cross_rows(active, grad_out)
        grad_pre = (matmul_rows(grad_out, weight_two.T) * silu_slope(before)).astype(jnp.bfloat16)
        grad_one = grad_one + cross_rows(differ, grad_pre)
        grad_bias = grad_bias + lax.optimization_barrier(jnp.sum(grad_pre.astype(jnp.float32).reshape(-1, feat_width), 0))
        grad_feat = grad_feat + spread_diff(matmul_rows(grad_pre, weight_one.T), dim_no)
    return (grad_feat, grad_one, grad_two, grad_bias)

def node_forward(features, summed, weight_in, weight_out, bias_node):
    joined = jnp.concatenate([features, summed.astype(jnp.bfloat16)], -1)
    before = matmul_rows(joined, weight_in) + bias_node
    active = jax.nn.silu(before).astype(jnp.bfloat16)
    result = (features.astype(jnp.float32) + matmul_rows(active, weight_out)).astype(jnp.bfloat16)
    return (result, (joined, before, active))

def node_backward(grad_next, stored, weight_in, weight_out):
    joined, before, active = stored
    feat_width = grad_next.shape[-1]
    grad_out_w = cross_rows(active, grad_next)
    grad_pre = (matmul_rows(grad_next, weight_out.T) * silu_slope(before)).astype(jnp.bfloat16)
    grad_in_w = cross_rows(joined, grad_pre)
    grad_bias = lax.optimization_barrier(jnp.sum(grad_pre.astype(jnp.float32).reshape(-1, feat_width), 0))
    grad_joined = matmul_rows(grad_pre, weight_in.T)
    grad_feat = grad_next.astype(jnp.float32) + grad_joined[..., :feat_width]
    return (grad_feat, grad_joined[..., feat_width:], grad_in_w, grad_out_w, grad_bias)

def couple(array, elem_dim, node_dim):
    moved = jnp.moveaxis(array, (elem_dim, node_dim), (0, 1))
    front_face = moved[:, 0]
    back_face = moved[:, -1]
    zero_face = jnp.zeros_like(front_face[:1])
    new_front = front_face + jnp.concatenate([zero_face, back_face[:-1]], 0)
    new_back = back_face + jnp.concatenate([front_face[1:], zero_face], 0)
    joined = jnp.concatenate([new_front[:, None], moved[:, 1:-1], new_back[:, None]], 1)
    return jnp.moveaxis(joined, (0, 1), (elem_dim, node_dim))

def couple_all(array):
    full_shape = array.shape
    along_x = couple(array.reshape((N_GX * EB, NODE) + full_shape[1:]), 0, 1).reshape(full_shape)
    along_y = couple(along_x.reshape(full_shape[:1] + (N_GY * EB, NODE) + full_shape[2:]), 1, 2).reshape(full_shape)
    return couple(along_y, 2, 3)

def reference(state, cotangent, counts, edge_weights, node_in, node_out, biases):
    layer_total = LAYERS_ALL
    slot_place = jnp.arange(N_GZ * LZ, dtype=jnp.int32)
    owner_dev = slot_place // LZ
    within = slot_place % LZ
    starts = (jnp.cumsum(counts) - counts).astype(jnp.int32)
    target = jnp.where(within < counts[owner_dev], starts[owner_dev] + within, layer_total).astype(jnp.int32)

    def compact(array):
        holder = jnp.zeros(array.shape[:2] + (layer_total + 1,) + array.shape[3:], array.dtype)
        return holder.at[:, :, target].set(array)[:, :, :layer_total]

    def expand(array):
        padded = jnp.concatenate([array, jnp.zeros_like(array[:, :, :1])], 2)
        return padded[:, :, target]
    features = compact(state)
    grad_next = compact(cotangent)
    grid_shape = features.shape[:4]

    def to_cells(array):
        return array.reshape((N_GX * EB, NODE, N_GY * EB, NODE, layer_total, NODE, array.shape[-1]))

    def to_grid(array):
        return array.reshape(grid_shape + (array.shape[-1],))
    copies = couple_all(jnp.ones(grid_shape + (1,), jnp.float32))
    saved = []
    for layer_no in range(2):
        messages, edge_store = edges_forward(to_cells(features), edge_weights[layer_no, 0], edge_weights[layer_no, 1], biases[layer_no, 0])
        summed = couple_all(to_grid(messages)) / copies
        result, node_store = node_forward(features, summed, node_in[layer_no], node_out[layer_no], biases[layer_no, 1])
        saved.append((edge_store, node_store))
        features = result
    per_layer = [None, None]
    for layer_no in (1, 0):
        edge_store, node_store = saved[layer_no]
        grad_feat, grad_sum, grad_in_w, grad_out_w, grad_node_b = node_backward(grad_next, node_store, node_in[layer_no], node_out[layer_no])
        grad_msg = couple_all(grad_sum / copies)
        grad_edge, grad_one, grad_two, grad_edge_b = edges_backward(to_cells(grad_msg), edge_store, edge_weights[layer_no, 0], edge_weights[layer_no, 1])
        grad_next = (grad_feat + to_grid(grad_edge)).astype(jnp.bfloat16)
        per_layer[layer_no] = (jnp.stack([grad_one, grad_two]), grad_in_w, grad_out_w, jnp.stack([grad_edge_b, grad_node_b]))
    grad_scale = 1.0 / math.sqrt(NODES_ALL)
    edge_grads = jnp.stack([per_layer[0][0], per_layer[1][0]]) * grad_scale
    node_in_grad = jnp.stack([per_layer[0][1], per_layer[1][1]]) * grad_scale
    node_out_grad = jnp.stack([per_layer[0][2], per_layer[1][2]]) * grad_scale
    bias_grads = jnp.stack([per_layer[0][3], per_layer[1][3]]) * grad_scale
    return (expand(grad_next), edge_grads, node_in_grad, node_out_grad, bias_grads)
```

```python
import functools
import math

import jax
import jax.numpy as jnp
from jax import lax
from jax.experimental import pallas as pl
from jax.experimental.pallas import tpu as pltpu
from jax.sharding import PartitionSpec as P

F32 = jnp.float32
BF16 = jnp.bfloat16
H = 128
ROWS = 768
MESH = pl.DeviceIdType.MESH


def mm(a, b):
    return jnp.dot(a, b, preferred_element_type=F32)


def mm_rows(a, b):
    return lax.dot_general(a, b, (((0,), (0,)), ((), ())), preferred_element_type=F32)


def act(pre):
    sig = 0.5 * jnp.tanh(0.5 * pre) + 0.5
    value = pre * sig
    return value, sig + value - value * sig


def flat(x):
    return x.reshape(256, x.shape[-1])


def kernel(
    sizes,
    scale,
    state,
    cotangent,
    counts,
    edge_w,
    node_in,
    node_out,
    biases,
    state_grad,
    edge_grads,
    node_in_grad,
    node_out_grad,
    bias_grads,
    w_first,
    w_agg,
    w_out_t,
    w_in_t,
    w_two_t,
    w_one_t,
    h_one,
    g_mid,
    pre_a,
    pre_n,
    field,
    dh,
    slope_x,
    slope_y,
    slope_z,
    slope_n,
    spread,
    agg,
    active,
    inv_yz,
    carry,
    pbuf,
    dbuf,
    hilo,
    bias_acc,
    gbuf,
    x_in,
    y_in,
    z_out,
    z_in,
    red_y,
    sum_y,
    red_x,
    sum_x,
    red_z,
    sum_z,
    gat_x,
    gat_y,
    ex_send,
    ex_recv,
    ar_send,
    ar_recv,
):
    n_x, n_y, n_z = sizes
    i_x, i_y, i_z = lax.axis_index("gx"), lax.axis_index("gy"), lax.axis_index("gz")
    here = {"gx": i_x, "gy": i_y, "gz": i_z}
    size = {"gx": n_x, "gy": n_y, "gz": n_z}

    def peer(axis, d):
        return lax.rem(here[axis] + d, size[axis])

    def at_axis(axis, d):
        q = peer(axis, d)
        return tuple(q if name == axis else here[name] for name in ("gx", "gy", "gz"))

    barrier = pltpu.get_barrier_semaphore()
    for axis in ("gx", "gy", "gz"):
        for d in range(1, size[axis]):
            pl.semaphore_signal(barrier, inc=1, device_id=at_axis(axis, d), device_id_type=MESH)
    pl.semaphore_wait(barrier, n_x + n_y + n_z - 3)

    def flag(cond):
        return jnp.where(cond, 1.0, 0.0).astype(F32)

    live = flag(counts[0] > 1)
    left = {axis: flag(here[axis] > 0) for axis in here}
    right = {axis: flag(here[axis] < size[axis] - 1) for axis in here}

    sk = lax.broadcasted_iota(jnp.int32, (16, H), 0)
    one = jnp.ones((16, H), F32)
    zero = jnp.zeros((16, H), F32)
    row_live = jnp.where(sk < 8, one, one * live)
    not_top = jnp.where((sk == 7) | (sk == 15), zero, one)
    bottom = jnp.where(sk == 0, one, zero)
    top = jnp.where(sk == 7, one * (1.0 - live), jnp.where(sk == 15, one * live, zero))
    mult_z = (
        one
        + jnp.where(sk == 0, one * left["gz"], zero)
        + jnp.where(sk == 8, one, zero)
        + jnp.where(sk == 7, one * jnp.maximum(live, right["gz"]), zero)
        + jnp.where(sk == 15, one * right["gz"], zero)
    )
    for y in range(16):
        mult_y = {0: left["gy"], 7: 1.0, 8: 1.0, 15: right["gy"]}.get(y, 0.0)
        inv_yz[y] = 1.0 / (mult_z * (1.0 + mult_y))

    def inv_x(p):
        extra = (
            flag(p == 0) * left["gx"]
            + flag((p == 7) | (p == 8))
            + flag(p == 15) * right["gx"]
        )
        return 1.0 - 0.5 * extra

    def turn(w):
        return w.astype(F32).T.astype(BF16)

    for l in range(2):
        w_first[l] = jnp.concatenate([edge_w[l, 0], node_in[l, :H]], 1)
        w_agg[l] = node_in[l, H:]
        w_out_t[l] = turn(node_out[l])
        w_in_t[l] = jnp.concatenate([turn(node_in[l, :H]), turn(node_in[l, H:])], 1)
        two_t = turn(edge_w[l, 1])
        w_two_t[l] = jnp.concatenate([two_t, two_t], 0)
        w_one_t[l] = turn(edge_w[l, 0])
    gbuf[...] = jnp.zeros_like(gbuf)
    bias_acc[...] = jnp.zeros_like(bias_acc)

    def roll_up(x):
        return pltpu.roll(x.reshape(16, 8, H), 7, 1).reshape(8, 16, H)

    def roll_down(x):
        return pltpu.roll(x.reshape(16, 8, H), 1, 1).reshape(8, 16, H)

    def spread_y(u):
        pad = jnp.zeros((1, 16, H), F32)
        return jnp.concatenate([pad, u], 0) - jnp.concatenate([u, pad], 0)

    def put_first(l, p, h_plane):
        both = mm(h_plane, w_first[l])
        pre_a[p] = both[:, :H].reshape(16, 16, H)
        pre_n[p] = both[:, H:].reshape(16, 16, H)

    def put_field(p, r):
        r = r.reshape(16, 16, H) * row_live
        low, high = r[:, :8], r[:, 8:]
        k = lax.broadcasted_iota(jnp.int32, (16, 8, H), 1)
        none = jnp.zeros((16, 8, H), F32)
        low2 = low + jnp.where(k == 7, pltpu.roll(high, 7, 1), none)
        high2 = high + jnp.where(k == 0, pltpu.roll(low, 1, 1), none)
        r = jnp.concatenate([low2, high2], 1)
        joint = r[7:8] + r[8:9]
        field[p] = jnp.concatenate([r[:7], joint, joint, r[9:]], 0)

    def messages(l):
        carry[...] = jnp.zeros_like(carry)
        bias = biases[l, 0:1]

        def step(p, _):
            nxt = jnp.minimum(p + 1, 15)
            inner = 1.0 - flag(lax.rem(p, 8) == 7)
            for e in (0, 1):
                ys = slice(8 * e, 8 * e + 8)
                mine = pre_a[p, ys]
                biased = mine - bias
                ux, sx = act(pre_a[nxt, ys] - biased)
                ux = ux * inner
                slope_x[l, p, ys] = sx * inner
                total = carry[ys] - ux
                carry[ys] = ux
                uy, sy = act(mine[1:] - biased[:7])
                slope_y[l, p, 8 * e : 8 * e + 7] = sy
                total = total + spread_y(uy)
                uz, sz = act(roll_up(mine) - biased)
                uz = uz * not_top
                slope_z[l, p, ys] = sz * not_top
                total = total + roll_down(uz) - uz
                spread[l, p, ys] = total.astype(BF16)
            put_field(p, mm(flat(spread[l, p]), edge_w[l, 1]))
            return 0

        lax.fori_loop(0, 16, step, 0)

    def join_x():
        joint = field[7] + field[8]
        field[7] = joint
        field[8] = joint

    def remote(src, dst, n, axis, d, send, recv):
        return pltpu.make_async_remote_copy(
            src_ref=src,
            dst_ref=dst,
            send_sem=send.at[n],
            recv_sem=recv.at[n],
            device_id=at_axis(axis, d),
            device_id_type=MESH,
        )

    def exchange(e):
        join_x()
        sends = [
            remote(field.at[0], x_in.at[e, 1], 6 * e, "gx", n_x - 1, ex_send, ex_recv),
            remote(field.at[15], x_in.at[e, 0], 6 * e + 1, "gx", 1, ex_send, ex_recv),
        ]
        for s in sends:
            s.start()
        for s in sends:
            s.wait()
        field[0] = field[0] + x_in[e, 0] * left["gx"]
        field[15] = field[15] + x_in[e, 1] * right["gx"]
        sends = [
            remote(field.at[:, 0], y_in.at[e, 1], 6 * e + 2, "gy", n_y - 1, ex_send, ex_recv),
            remote(field.at[:, 15], y_in.at[e, 0], 6 * e + 3, "gy", 1, ex_send, ex_recv),
        ]
        for s in sends:
            s.start()
        for s in sends:
            s.wait()

        def edge(p, _):
            field[p, 0] = field[p, 0] + y_in[e, 0, p] * left["gy"]
            field[p, 15] = field[p, 15] + y_in[e, 1, p] * right["gy"]
            z_out[e, 0, p] = field[p, :, 0, :]
            z_out[e, 1, p] = field[p, :, 7, :] * (1.0 - live) + field[p, :, 15, :] * live
            return 0

        lax.fori_loop(0, 16, edge, 0)
        sends = [
            remote(z_out.at[e, 0], z_in.at[e, 1], 6 * e + 4, "gz", n_z - 1, ex_send, ex_recv),
            remote(z_out.at[e, 1], z_in.at[e, 0], 6 * e + 5, "gz", 1, ex_send, ex_recv),
        ]
        for s in sends:
            s.start()
        for s in sends:
            s.wait()

    bottom_in = bottom * left["gz"]
    top_in = top * right["gz"]

    def summed(e, p):
        below = z_in[e, 0, p][:, None, :]
        above = z_in[e, 1, p][:, None, :]
        return field[p] + below * bottom_in + above * top_in

    def node(l, e, p, h_plane):
        a = (summed(e, p) * (inv_yz[...] * inv_x(p))).astype(BF16)
        agg[l, p] = a
        pre = mm(flat(a), w_agg[l]) + flat(pre_n[p]) + biases[l, 1:2]
        v, slope = act(pre)
        v = v.astype(BF16)
        active[l, p] = v.reshape(16, 16, H)
        return v, slope

    def node_back(l, p, h_plane, g, slope):
        dpn = mm(g, w_out_t[l]) * slope
        bias_acc[l, 1] = bias_acc[l, 1] + jnp.sum(dpn.reshape(16, 16, H), 0)
        dpn = dpn.astype(BF16)
        gbuf[l, 512:640] += mm_rows(flat(active[l, p]), g)
        gbuf[l, 256:384] += mm_rows(h_plane, dpn)
        gbuf[l, 384:512] += mm_rows(flat(agg[l, p]), dpn)
        dx = mm(dpn, w_in_t[l])
        dh[p] = (g.astype(F32) + dx[:, :H]).reshape(16, 16, H)
        r = dx[:, H:].reshape(16, 16, H) * (inv_yz[...] * inv_x(p))
        put_field(p, r)

    def edge_first(l, e):
        def step(p, _):
            dr = flat(summed(e, p) * row_live)
            hi = dr.astype(BF16)
            lo = (dr - hi.astype(F32)).astype(BF16)
            pair = jnp.concatenate([hi, lo], 1)
            pre_a[p] = mm(pair, w_two_t[l]).reshape(16, 16, H)
            both = mm_rows(flat(spread[l, p]), pair)
            gbuf[l, 128:256] += both[:, :H] + both[:, H:]
            return 0

        lax.fori_loop(0, 16, step, 0)

    def edge_back(l, p, h_plane):
        nxt = jnp.minimum(p + 1, 15)
        for e in (0, 1):
            ys = slice(8 * e, 8 * e + 8)
            mine = pre_a[p, ys]
            dx = (pre_a[nxt, ys] - mine) * slope_x[l, p, ys]
            total = carry[ys] - dx
            carry[ys] = dx
            dy = (mine[1:] - mine[:7]) * slope_y[l, p, 8 * e : 8 * e + 7]
            total = total + spread_y(dy)
            dz = (roll_up(mine) - mine) * slope_z[l, p, ys]
            total = total + roll_down(dz) - dz
            bias_acc[l, 0] = bias_acc[l, 0] + (
                jnp.sum(dx, 0) + jnp.sum(dy, 0) + jnp.sum(dz, 0)
            )
            pbuf[ys] = total.astype(BF16)
        back = flat(pbuf[...])
        gbuf[l, 0:128] += mm_rows(h_plane, back)
        return (flat(dh[p]) + mm(back, w_one_t[l])).astype(BF16)

    def start_all(copies):
        for c in copies:
            c.start()
        return copies

    def wait_all(copies):
        for c in copies:
            c.wait()

    part_y, part_x = ROWS // n_y, ROWS // n_y // n_x
    first_z = n_y - 1 + n_x - 1
    first_gx = first_z + n_z - 1
    first_gy = first_gx + n_x - 1

    def ar_one(l):
        return start_all([
            remote(
                gbuf.at[l, pl.ds(pl.multiple_of(peer("gy", d) * part_y, 8), part_y)],
                red_y.at[l, d - 1], d - 1, "gy", d, ar_send.at[l], ar_recv.at[l],
            )
            for d in range(1, n_y)
        ])

    def ar_two(l, sent):
        wait_all(sent)
        total = gbuf[l, pl.ds(pl.multiple_of(i_y * part_y, 8), part_y)]
        for d in range(1, n_y):
            total = total + red_y[l, d - 1]
        sum_y[l] = total
        return start_all([
            remote(
                sum_y.at[l, pl.ds(pl.multiple_of(peer("gx", d) * part_x, 8), part_x)],
                red_x.at[l, d - 1], n_y - 2 + d, "gx", d, ar_send.at[l], ar_recv.at[l],
            )
            for d in range(1, n_x)
        ])

    def ar_three(l, sent):
        wait_all(sent)
        total = sum_y[l, pl.ds(pl.multiple_of(i_x * part_x, 8), part_x)]
        for d in range(1, n_x):
            total = total + red_x[l, d - 1]
        sum_x[l] = total
        red_z[l, i_z] = total
        return start_all([
            remote(
                sum_x.at[l], red_z.at[l, i_z], first_z + d - 1, "gz", d,
                ar_send.at[l], ar_recv.at[l],
            )
            for d in range(1, n_z)
        ])

    def ar_four(l, sent):
        wait_all(sent)
        total = red_z[l, 0]
        for d in range(1, n_z):
            total = total + red_z[l, d]
        total = total * scale
        sum_z[l] = total
        gat_x[l, pl.ds(pl.multiple_of(i_x * part_x, 8), part_x)] = total
        return start_all([
            remote(
                sum_z.at[l], gat_x.at[l, pl.ds(pl.multiple_of(i_x * part_x, 8), part_x)],
                first_gx + d - 1, "gx", d, ar_send.at[l], ar_recv.at[l],
            )
            for d in range(1, n_x)
        ])

    def ar_five(l, sent):
        wait_all(sent)
        gat_y[l, pl.ds(pl.multiple_of(i_y * part_y, 8), part_y)] = gat_x[l]
        return start_all([
            remote(
                gat_x.at[l], gat_y.at[l, pl.ds(pl.multiple_of(i_y * part_y, 8), part_y)],
                first_gy + d - 1, "gy", d, ar_send.at[l], ar_recv.at[l],
            )
            for d in range(1, n_y)
        ])

    def ar_last(l, sent):
        wait_all(sent)
        edge_grads[l, 0] = gat_y[l, 0:128]
        edge_grads[l, 1] = gat_y[l, 128:256]
        node_in_grad[l] = gat_y[l, 256:512]
        node_out_grad[l] = gat_y[l, 512:640]
        bias_grads[l] = gat_y[l, 640:642]

    def finish_bias(l):
        gbuf[l, 640:641] = jnp.sum(bias_acc[l, 0], 0, keepdims=True)
        gbuf[l, 641:642] = jnp.sum(bias_acc[l, 1], 0, keepdims=True)

    def first(p, _):
        put_first(0, p, flat(state[p]))
        return 0

    lax.fori_loop(0, 16, first, 0)
    messages(0)
    exchange(0)

    def middle(p, _):
        h_plane = flat(state[p])
        v, slope = node(0, 0, p, h_plane)
        slope_n[p] = slope.reshape(16, 16, H)
        nxt = (h_plane.astype(F32) + mm(v, node_out[0])).astype(BF16)
        h_one[p] = nxt.reshape(16, 16, H)
        put_first(1, p, nxt)
        return 0

    lax.fori_loop(0, 16, middle, 0)
    messages(1)
    exchange(1)

    def last(p, _):
        h_plane = flat(h_one[p])
        v, slope = node(1, 1, p, h_plane)
        g = flat((cotangent[p].astype(F32) * row_live).astype(BF16))
        node_back(1, p, h_plane, g, slope)
        return 0

    lax.fori_loop(0, 16, last, 0)
    exchange(2)
    edge_first(1, 2)
    carry[...] = jnp.zeros_like(carry)

    def turnover(p, _):
        g = edge_back(1, p, flat(h_one[p]))
        node_back(0, p, flat(state[p]), g, flat(slope_n[p]))
        return 0

    lax.fori_loop(0, 16, turnover, 0)
    finish_bias(1)
    sent = ar_one(1)
    exchange(3)
    sent = ar_two(1, sent)
    edge_first(0, 3)
    sent = ar_three(1, sent)
    carry[...] = jnp.zeros_like(carry)

    def final(p, _):
        g = edge_back(0, p, flat(state[p]))
        state_grad[p] = g.reshape(16, 16, H)
        return 0

    lax.fori_loop(0, 16, final, 0)
    finish_bias(0)
    sent0 = ar_one(0)
    sent = ar_four(1, sent)
    sent0 = ar_two(0, sent0)
    sent = ar_five(1, sent)
    sent0 = ar_three(0, sent0)
    ar_last(1, sent)
    sent0 = ar_four(0, sent0)
    sent0 = ar_five(0, sent0)
    ar_last(0, sent0)


def on_device(sizes, state, cotangent, counts, edge_weights, node_in, node_out, biases):
    n_x, n_y, n_z = sizes
    shape = state.shape
    nodes = (shape[0] * n_x) * (shape[1] * n_y) * (3 * shape[2] * n_z // 4) * shape[3]
    planes = (shape[0], shape[1], shape[2] * shape[3], H)
    part_y, part_x = ROWS // n_y, ROWS // n_y // n_x
    n_ar = 2 * (n_x - 1) + 2 * (n_y - 1) + n_z - 1
    vmem = pl.BlockSpec(memory_space=pltpu.VMEM)
    scratch = [
        pltpu.VMEM((2, H, 2 * H), BF16),
        pltpu.VMEM((2, H, H), BF16),
        pltpu.VMEM((2, H, H), BF16),
        pltpu.VMEM((2, H, 2 * H), BF16),
        pltpu.VMEM((2, 2 * H, H), BF16),
        pltpu.VMEM((2, H, H), BF16),
        pltpu.VMEM(planes, BF16),
        pltpu.VMEM((8, H), BF16),
        pltpu.VMEM(planes, F32),
        pltpu.VMEM(planes, F32),
        pltpu.VMEM(planes, F32),
        pltpu.VMEM(planes, F32),
        pltpu.VMEM((2,) + planes, F32),
        pltpu.VMEM((2,) + planes, F32),
        pltpu.VMEM((2,) + planes, F32),
        pltpu.VMEM(planes, F32),
        pltpu.VMEM((2,) + planes, BF16),
        pltpu.VMEM((2,) + planes, BF16),
        pltpu.VMEM((2,) + planes, BF16),
        pltpu.VMEM(planes[1:], F32),
        pltpu.VMEM(planes[1:], F32),
        pltpu.VMEM(planes[1:], BF16),
        pltpu.VMEM((8, H), BF16),
        pltpu.VMEM((8, H), BF16),
        pltpu.VMEM((2, 2, 16, H), F32),
        pltpu.VMEM((2, ROWS, H), F32),
        pltpu.VMEM((4, 2) + planes[1:], F32),
        pltpu.VMEM((4, 2, 16, 16, H), F32),
        pltpu.VMEM((4, 2, 16, 16, H), F32),
        pltpu.VMEM((4, 2, 16, 16, H), F32),
        pltpu.VMEM((2, n_y - 1, part_y, H), F32),
        pltpu.VMEM((2, part_y, H), F32),
        pltpu.VMEM((2, n_x - 1, part_x, H), F32),
        pltpu.VMEM((2, part_x, H), F32),
        pltpu.VMEM((2, n_z, part_x, H), F32),
        pltpu.VMEM((2, part_x, H), F32),
        pltpu.VMEM((2, part_y, H), F32),
        pltpu.VMEM((2, ROWS, H), F32),
        pltpu.SemaphoreType.DMA((24,)),
        pltpu.SemaphoreType.DMA((24,)),
        pltpu.SemaphoreType.DMA((2, n_ar)),
        pltpu.SemaphoreType.DMA((2, n_ar)),
    ]
    outs = pl.pallas_call(
        functools.partial(kernel, sizes, 1.0 / math.sqrt(nodes)),
        out_shape=(
            jax.ShapeDtypeStruct(planes, BF16),
            jax.ShapeDtypeStruct((2, 2, H, H), F32),
            jax.ShapeDtypeStruct((2, 2 * H, H), F32),
            jax.ShapeDtypeStruct((2, H, H), F32),
            jax.ShapeDtypeStruct((2, 2, H), F32),
        ),
        in_specs=[vmem, vmem, pl.BlockSpec(memory_space=pltpu.SMEM), vmem, vmem, vmem, vmem],
        out_specs=(vmem,) * 5,
        scratch_shapes=scratch,
        compiler_params=pltpu.CompilerParams(
            collective_id=0, has_side_effects=True, vmem_limit_bytes=66_000_000
        ),
        name="layers",
    )(
        state.reshape(planes),
        cotangent.reshape(planes),
        counts,
        edge_weights,
        node_in,
        node_out,
        biases,
    )
    return (outs[0].reshape(shape),) + tuple(outs[1:])


def solution(mesh):
    sizes = tuple(mesh.shape[name] for name in ("gx", "gy", "gz"))
    grid = P("gx", "gy", "gz", None, None)
    return jax.shard_map(
        functools.partial(on_device, sizes),
        mesh=mesh,
        in_specs=(grid, grid, P("gz"), P(), P(), P(), P()),
        out_specs=(grid, P(), P(), P(), P()),
        check_vma=False,
    )
```

```python
import functools
import math

import jax
import jax.numpy as jnp
from jax import lax
from jax.experimental import pallas as pl
from jax.experimental.pallas import tpu as pltpu
from jax.sharding import PartitionSpec as P

F32 = jnp.float32
BF16 = jnp.bfloat16
H = 128
MESH = pl.DeviceIdType.MESH
AXES = ("gx", "gy", "gz")
UNITS = (768, 768, 256)
GROUPS = ((0, 1), (1, 5), (5, 8))


def mm(a, b):
    return jnp.dot(a, b, preferred_element_type=F32)


def mm_rows(a, b):
    return lax.dot_general(a, b, (((0,), (0,)), ((), ())), preferred_element_type=F32)


def act(x):
    t = jnp.tanh(x)
    m = x * t
    return x + m, (1.0 + t) * ((1.0 + x) - m)


def flat(x):
    return x.reshape(-1, x.shape[-1])


def kernel(sizes, scale, *refs):
    (
        state, cotangent, counts, edge_w, node_in, node_out, biases,
        state_grad, edge_grads, node_in_grad, node_out_grad, bias_grads,
        w_first, w_agg, w_out_t, w_in_t, w_two_t, w_one_t, half_bias,
        h_one, g_now, d_now, p_now, pre_a, pre_n, field, dh,
        slope_x, slope_y, slope_z, slope_n, spread, agg, active, inv_yz, carry, bias_acc,
        x_in, y_out, y_in, z_out, z_in, yz_out, yz_in, ex_send, ex_recv,
    ) = refs[:46]
    units = [refs[46 + 11 * u : 57 + 11 * u] for u in range(3)]
    n_x, n_y, n_z = sizes
    i_x, i_y, i_z = (lax.axis_index(name) for name in AXES)
    here = dict(zip(AXES, (i_x, i_y, i_z)))
    size = dict(zip(AXES, sizes))

    def peer(axis, d):
        return lax.rem(here[axis] + d, size[axis])

    def device(**moves):
        return tuple(peer(a, moves[a] % size[a]) if a in moves else here[a] for a in AXES)

    barrier = pltpu.get_barrier_semaphore()
    partners = [device(**{a: d}) for a in AXES for d in range(1, size[a])]
    partners += [device(gy=dy, gz=dz) for dy in (-1, 1) for dz in (-1, 1)]
    for q in partners:
        pl.semaphore_signal(barrier, inc=1, device_id=q, device_id_type=MESH)
    pl.semaphore_wait(barrier, len(partners))

    def flag(cond):
        return jnp.where(cond, 1.0, 0.0).astype(F32)

    live = flag(counts[0] > 1)
    left = {a: flag(here[a] > 0) for a in AXES}
    right = {a: flag(here[a] < size[a] - 1) for a in AXES}

    sk = lax.broadcasted_iota(jnp.int32, (16, H), 0)
    one = jnp.ones((16, H), F32)
    zero = jnp.zeros((16, H), F32)
    row_live = jnp.where(sk < 8, one, one * live)
    not_top = jnp.where((sk == 7) | (sk == 15), zero, one)
    bottom = jnp.where(sk == 0, one, zero)
    top = jnp.where(sk == 7, one * (1.0 - live), jnp.where(sk == 15, one * live, zero))
    bottom_in = bottom * left["gz"]
    top_in = top * right["gz"]
    first_y = bottom * left["gy"]
    last_y = jnp.where(sk == 15, one * right["gy"], zero)
    mult_z = (
        one
        + jnp.where(sk == 0, one * left["gz"], zero)
        + jnp.where(sk == 8, one, zero)
        + jnp.where(sk == 7, one * jnp.maximum(live, right["gz"]), zero)
        + jnp.where(sk == 15, one * right["gz"], zero)
    )
    for y in range(16):
        mult_y = {0: left["gy"], 7: 1.0, 8: 1.0, 15: right["gy"]}.get(y, 0.0)
        inv_yz[y] = 1.0 / (mult_z * (1.0 + mult_y))

    def plane(t, side):
        return 15 - t if side else t

    def inv_x(t, side):
        outer = right["gx"] if side else left["gx"]
        return 1.0 - 0.5 * (flag(t == 0) * outer + flag(t == 7))

    def turn(w):
        return w.astype(F32).T.astype(BF16)

    def half(w):
        return (w.astype(F32) * 0.5).astype(BF16)

    for l in range(2):
        w_first[l] = half(jnp.concatenate([edge_w[l, 0], node_in[l, :H]], 1))
        w_agg[l] = half(node_in[l, H:])
        w_out_t[l] = half(turn(node_out[l]))
        w_in_t[l] = jnp.concatenate([turn(node_in[l, :H]), turn(node_in[l, H:])], 1)
        two_t = half(turn(edge_w[l, 1]))
        w_two_t[l] = jnp.concatenate([two_t, two_t], 0)
        w_one_t[l] = turn(edge_w[l, 0])
    half_bias[...] = biases[...] * 0.5
    for u in units:
        u[0][...] = jnp.zeros_like(u[0])
    bias_acc[...] = jnp.zeros_like(bias_acc)

    at_one = ((2, 0), (0, 0))
    at_two = ((1, 0), (0, 128))
    at_in = ((1, 128), (0, 256))
    at_out = ((1, 384), (0, 512))
    at_bias = (((2, 128), (1, 512)), ((0, 640), (0, 641)))

    def add_grad(place, shift, value):
        u, row = place
        units[u][0][row + shift : row + shift + value.shape[0]] += value

    def steps(order, body, before=None, after=None):
        before, after = before or {}, after or {}

        def step(i, _):
            for k, todo in before.items():
                pl.when(i == k)(todo)
            body(order(i))
            for k, todo in after.items():
                pl.when(i == k)(todo)
            return 0

        lax.fori_loop(0, 8, step, 0)

    def ascending(i):
        return i

    def first_last(i):
        return lax.rem(i + 1, 8)

    def first_middle(i):
        late = lax.div(i, 4)
        return (1 - late) * (i + 1) + late * i * lax.div(i + 3, 8)

    def roll_up(x):
        return pltpu.roll(x.reshape(16, 8, H), 7, 1).reshape(8, 16, H)

    def roll_down(x):
        return pltpu.roll(x.reshape(16, 8, H), 1, 1).reshape(8, 16, H)

    def spread_y(u):
        pad = jnp.zeros((1, 16, H), F32)
        return jnp.concatenate([pad, u], 0) - jnp.concatenate([u, pad], 0)

    def put_first(l, p, h_plane):
        both = mm(h_plane, w_first[l])
        pre_a[p] = both[:, :H].reshape(16, 16, H)
        pre_n[p] = both[:, H:].reshape(16, 16, H)

    def put_field(p, r):
        r = r.reshape(16, 16, H) * row_live
        low, high = r[:, :8], r[:, 8:]
        k = lax.broadcasted_iota(jnp.int32, (16, 8, H), 1)
        none = jnp.zeros((16, 8, H), F32)
        low2 = low + jnp.where(k == 7, pltpu.roll(high, 7, 1), none)
        high2 = high + jnp.where(k == 0, pltpu.roll(low, 1, 1), none)
        r = jnp.concatenate([low2, high2], 1)
        joint = r[7:8] + r[8:9]
        field[p] = jnp.concatenate([r[:7], joint, joint, r[9:]], 0)

    def remote(src, dst, sem, n, to):
        send, recv = sem
        return pltpu.make_async_remote_copy(
            src_ref=src,
            dst_ref=dst,
            send_sem=send.at[n],
            recv_sem=recv.at[n],
            device_id=to,
            device_id_type=MESH,
        )

    def start(copies):
        for c in copies:
            c.start()

    def wait(copies):
        for c in copies:
            c.wait()

    def x_copies(e):
        sem = (ex_send.at[e], ex_recv.at[e])
        return [
            remote(field.at[0], x_in.at[e, 1], sem, 0, device(gx=-1)),
            remote(field.at[15], x_in.at[e, 0], sem, 1, device(gx=1)),
        ]

    def group_copies(e, g):
        sem = (ex_send.at[e], ex_recv.at[e])
        at = pl.ds(2 * GROUPS[g][0], 2 * (GROUPS[g][1] - GROUPS[g][0]))
        n = 2 + 8 * g
        copies = []
        for f in (0, 1):
            move = 2 * f - 1
            copies.append(
                remote(y_out.at[e, f, at], y_in.at[e, 1 - f, at], sem, n + f, device(gy=move))
            )
            copies.append(
                remote(z_out.at[e, f, at], z_in.at[e, 1 - f, at], sem, n + 2 + f, device(gz=move))
            )
            for fy in (0, 1):
                copies.append(
                    remote(
                        yz_out.at[e, g, f, fy],
                        yz_in.at[e, g, 1 - f, 1 - fy],
                        sem,
                        n + 4 + 2 * f + fy,
                        device(gy=2 * fy - 1, gz=move),
                    )
                )
        return copies

    def line(t, side):
        g = lax.div(t + 3, 4)
        return g, 2 * (t + 3 - 4 * g) + side

    def pack(e, t):
        for side in (0, 1):
            p, s = plane(t, side), 2 * t + side
            g, row = line(t, side)
            y_out[e, 0, s] = field[p, 0]
            y_out[e, 1, s] = field[p, 15]
            for f in (0, 1):
                if f:
                    z = field[p, :, 7, :] * (1.0 - live) + field[p, :, 15, :] * live
                else:
                    z = field[p, :, 0, :]
                z_out[e, f, s] = z
                yz_out[e, g, f, 0, pl.ds(row, 1), :] = z[0:1]
                yz_out[e, g, f, 1, pl.ds(row, 1), :] = z[15:16]

    def send_x(e):
        return lambda: start(x_copies(e))

    def send(e, g):
        return lambda: start(group_copies(e, g))

    def take(e, g):
        return lambda: wait(group_copies(e, g))

    def join_middle(e):
        joint = field[7] + field[8]
        field[7] = joint
        field[8] = joint
        pack(e, 7)

    def take_x(e):
        wait(x_copies(e))
        field[0] = field[0] + x_in[e, 0] * left["gx"]
        field[15] = field[15] + x_in[e, 1] * right["gx"]
        pack(e, 0)

    def summed(e, t, side):
        p, s = plane(t, side), 2 * t + side
        g, row = line(t, side)
        z = []
        for f in (0, 1):
            z.append(
                z_in[e, f, s]
                + yz_in[e, g, f, 0, pl.ds(row, 1), :] * first_y
                + yz_in[e, g, f, 1, pl.ds(row, 1), :] * last_y
            )
        whole = field[p]
        whole = jnp.concatenate(
            [
                whole[0:1] + (y_in[e, 0, s] * left["gy"])[None],
                whole[1:15],
                whole[15:16] + (y_in[e, 1, s] * right["gy"])[None],
            ],
            0,
        )
        return whole + z[0][:, None, :] * bottom_in + z[1][:, None, :] * top_in

    def messages(l, e):
        carry[...] = jnp.zeros_like(carry)
        bias = half_bias[l, 0:1]

        def body(t):
            inner = 1.0 - flag(t == 7)
            for side in (0, 1):
                p = plane(t, side)
                nxt = jnp.maximum(14 - t, 8) if side else jnp.minimum(t + 1, 7)
                for q in (0, 1):
                    ys = slice(8 * q, 8 * q + 8)
                    mine = pre_a[p, ys]
                    biased = mine - bias
                    if side:
                        ux, sx = act((mine + bias) - pre_a[nxt, ys])
                    else:
                        ux, sx = act(pre_a[nxt, ys] - biased)
                    ux = ux * inner
                    slope_x[l, p, ys] = sx * inner
                    total = ux - carry[side, ys] if side else carry[side, ys] - ux
                    carry[side, ys] = ux
                    uy, sy = act(mine[1:] - biased[:7])
                    slope_y[l, p, 8 * q : 8 * q + 7] = sy
                    total = total + spread_y(uy)
                    uz, sz = act(roll_up(mine) - biased)
                    uz = uz * not_top
                    slope_z[l, p, ys] = sz * not_top
                    total = total + roll_down(uz) - uz
                    spread[l, p, ys] = total.astype(BF16)
                put_field(p, mm(flat(spread[l, p]), edge_w[l, 1]))
            pack(e, t)

        steps(ascending, body, after={0: send_x(e), 4: send(e, 1)})
        join_middle(e)
        send(e, 2)()
        take_x(e)
        send(e, 0)()

    def node(l, e, t, side):
        p = plane(t, side)
        a = (summed(e, t, side) * (inv_yz[...] * inv_x(t, side))).astype(BF16)
        agg[l, p] = a
        pre = mm(flat(a), w_agg[l]) + flat(pre_n[p]) + half_bias[l, 1:2]
        v, slope = act(pre)
        v = v.astype(BF16)
        active[l, p] = v.reshape(16, 16, H)
        return v, slope

    def node_back(l, t, side, g, slope):
        p = plane(t, side)
        dpn = mm(g, w_out_t[l]) * slope
        bias_acc[l, 1] = bias_acc[l, 1] + jnp.sum(dpn.reshape(16, 16, H), 0)
        dpn = dpn.astype(BF16)
        g_now[p] = g.reshape(16, 16, H)
        d_now[p] = dpn.reshape(16, 16, H)
        dx = mm(dpn, w_in_t[l])
        dh[p] = (g.astype(F32) + dx[:, :H]).reshape(16, 16, H)
        put_field(p, dx[:, H:].reshape(16, 16, H) * (inv_yz[...] * inv_x(t, side)))

    def by_fours(body):
        def step(i, _):
            body(pl.ds(4 * i, 4))
            return 0

        lax.fori_loop(0, 4, step, 0)

    def node_grads(l, h_ref):
        def body(at):
            d = flat(d_now[at])
            add_grad(at_out[l], 0, mm_rows(flat(active[l, at]), flat(g_now[at])))
            add_grad(at_in[l], 0, mm_rows(flat(h_ref[at]), d))
            add_grad(at_in[l], H, mm_rows(flat(agg[l, at]), d))

        by_fours(body)

    def first_grad(l, h_ref):
        by_fours(lambda at: add_grad(at_one[l], 0, mm_rows(flat(h_ref[at]), flat(p_now[at]))))

    def edge_first(l, e, after=None):
        def body(t):
            for side in (0, 1):
                p = plane(t, side)
                dr = flat(summed(e, t, side) * row_live)
                hi = dr.astype(BF16)
                lo = (dr - hi.astype(F32)).astype(BF16)
                pair = jnp.concatenate([hi, lo], 1)
                pre_a[p] = mm(pair, w_two_t[l]).reshape(16, 16, H)
                both = mm_rows(flat(spread[l, p]), pair)
                add_grad(at_two[l], 0, both[:, :H] + both[:, H:])

        steps(
            first_last,
            body,
            before={0: take(e, 1), 4: take(e, 2), 7: take(e, 0)},
            after=after,
        )

    def edge_back(l, t, side):
        p = plane(t, side)
        nxt = jnp.maximum(14 - t, 8) if side else jnp.minimum(t + 1, 7)
        for q in (0, 1):
            ys = slice(8 * q, 8 * q + 8)
            mine = pre_a[p, ys]
            if side:
                dx = (mine - pre_a[nxt, ys]) * slope_x[l, p, ys]
                total = dx - carry[side, ys]
            else:
                dx = (pre_a[nxt, ys] - mine) * slope_x[l, p, ys]
                total = carry[side, ys] - dx
            carry[side, ys] = dx
            dy = (mine[1:] - mine[:7]) * slope_y[l, p, 8 * q : 8 * q + 7]
            total = total + spread_y(dy)
            dz = (roll_up(mine) - mine) * slope_z[l, p, ys]
            total = total + roll_down(dz) - dz
            bias_acc[l, 0] = bias_acc[l, 0] + (
                jnp.sum(dx, 0) + jnp.sum(dy, 0) + jnp.sum(dz, 0)
            )
            p_now[p, ys] = total.astype(BF16)
        return (flat(dh[p]) + mm(flat(p_now[p]), w_one_t[l])).astype(BF16)

    def stage_copies(u, stage):
        (buf, red_y, sum_y, red_x, sum_x, red_z, sum_z, gat_x, gat_y, send_sem, recv_sem) = units[u]
        sem = (send_sem, recv_sem)
        part_y, part_x = UNITS[u] // n_y, UNITS[u] // n_y // n_x

        def part(index, rows):
            return pl.ds(pl.multiple_of(index * rows, 8), rows)

        if stage == 0:
            return [
                remote(buf.at[part(peer("gy", d), part_y)], red_y.at[d - 1], sem, d - 1, device(gy=d))
                for d in range(1, n_y)
            ]
        n = n_y - 2
        if stage == 1:
            return [
                remote(sum_y.at[part(peer("gx", d), part_x)], red_x.at[d - 1], sem, n + d, device(gx=d))
                for d in range(1, n_x)
            ]
        n += n_x - 1
        if stage == 2:
            return [
                remote(sum_x, red_z.at[i_z], sem, n + d, device(gz=d)) for d in range(1, n_z)
            ]
        n += n_z - 1
        if stage == 3:
            return [
                remote(sum_z, gat_x.at[part(i_x, part_x)], sem, n + d, device(gx=d))
                for d in range(1, n_x)
            ]
        n += n_x - 1
        return [
            remote(gat_x, gat_y.at[part(i_y, part_y)], sem, n + d, device(gy=d))
            for d in range(1, n_y)
        ]

    def reduce_step(u, stage):
        (buf, red_y, sum_y, red_x, sum_x, red_z, sum_z, gat_x, gat_y, _, _) = units[u]
        part_y, part_x = UNITS[u] // n_y, UNITS[u] // n_y // n_x
        mine_y = pl.ds(pl.multiple_of(i_y * part_y, 8), part_y)
        mine_x = pl.ds(pl.multiple_of(i_x * part_x, 8), part_x)

        def run():
            if stage > 0:
                wait(stage_copies(u, stage - 1))
            if stage == 1:
                total = buf[mine_y]
                for d in range(1, n_y):
                    total = total + red_y[d - 1]
                sum_y[...] = total
            if stage == 2:
                total = sum_y[mine_x]
                for d in range(1, n_x):
                    total = total + red_x[d - 1]
                sum_x[...] = total
                red_z[i_z] = total
            if stage == 3:
                total = red_z[0]
                for d in range(1, n_z):
                    total = total + red_z[d]
                total = total * scale
                sum_z[...] = total
                gat_x[mine_x] = total
            if stage == 4:
                gat_y[mine_y] = gat_x[...]
            if stage < 5:
                start(stage_copies(u, stage))

        return run

    def put_out(place, rows):
        u, row = place
        return units[u][8][row : row + rows]

    def finish_bias(l, kind):
        u, row = at_bias[l][kind]
        units[u][0][row : row + 1] = jnp.sum(bias_acc[l, kind], 0, keepdims=True)

    def first(t):
        for side in (0, 1):
            p = plane(t, side)
            put_first(0, p, flat(state[p]))

    steps(ascending, first)
    messages(0, 0)

    def middle(t):
        for side in (0, 1):
            p = plane(t, side)
            v, slope = node(0, 0, t, side)
            slope_n[p] = slope.reshape(16, 16, H)
            nxt = (flat(state[p]).astype(F32) + mm(v, node_out[0])).astype(BF16)
            h_one[p] = nxt.reshape(16, 16, H)
            put_first(1, p, nxt)

    steps(first_last, middle, before={0: take(0, 1), 4: take(0, 2), 7: take(0, 0)})
    messages(1, 1)

    def last(t):
        for side in (0, 1):
            p = plane(t, side)
            v, slope = node(1, 1, t, side)
            g = flat((cotangent[p].astype(F32) * row_live).astype(BF16))
            node_back(1, t, side, g, slope)
        pack(2, t)

    def after_outer():
        start(x_copies(2))
        start(group_copies(2, 1))

    steps(
        first_middle,
        last,
        before={0: take(1, 1), 4: take(1, 0), 5: take(1, 2)},
        after={4: after_outer},
    )
    join_middle(2)
    send(2, 2)()
    take_x(2)
    send(2, 0)()
    node_grads(1, h_one)
    edge_first(1, 2)
    carry[...] = jnp.zeros_like(carry)

    def turnover(t):
        for side in (0, 1):
            g = edge_back(1, t, side)
            node_back(0, t, side, g, flat(slope_n[plane(t, side)]))
        pack(3, t)

    steps(ascending, turnover, after={0: send_x(3), 4: send(3, 1)})
    join_middle(3)
    send(3, 2)()
    take_x(3)
    send(3, 0)()
    first_grad(1, h_one)
    finish_bias(1, 0)
    finish_bias(1, 1)
    reduce_step(0, 0)()
    node_grads(0, state)
    finish_bias(0, 1)
    edge_first(0, 3, after={1: reduce_step(0, 1)})
    reduce_step(1, 0)()
    reduce_step(0, 2)()
    carry[...] = jnp.zeros_like(carry)

    def final(t):
        for side in (0, 1):
            p = plane(t, side)
            g = edge_back(0, t, side)
            state_grad[p] = g.reshape(16, 16, H)
            add_grad(at_one[0], 0, mm_rows(flat(state[p]), flat(p_now[p])))

    steps(
        ascending,
        final,
        after={2: reduce_step(1, 1), 4: reduce_step(0, 3), 7: reduce_step(1, 2)},
    )
    finish_bias(0, 0)
    reduce_step(2, 0)()
    reduce_step(0, 4)()
    reduce_step(2, 1)()
    reduce_step(1, 3)()
    reduce_step(2, 2)()
    reduce_step(1, 4)()
    reduce_step(2, 3)()
    reduce_step(0, 5)()
    reduce_step(1, 5)()
    for l in range(2):
        edge_grads[l, 1] = put_out(at_two[l], H)
        node_in_grad[l] = put_out(at_in[l], 2 * H)
        node_out_grad[l] = put_out(at_out[l], H)
    reduce_step(2, 4)()
    reduce_step(2, 5)()
    for l in range(2):
        edge_grads[l, 0] = put_out(at_one[l], H)
        for kind in (0, 1):
            bias_grads[l, kind : kind + 1] = put_out(at_bias[l][kind], 1)


def on_device(sizes, state, cotangent, counts, edge_weights, node_in, node_out, biases):
    n_x, n_y, n_z = sizes
    shape = state.shape
    nodes = (shape[0] * n_x) * (shape[1] * n_y) * (3 * shape[2] * n_z // 4) * shape[3]
    planes = (shape[0], shape[1], shape[2] * shape[3], H)
    vmem = pl.BlockSpec(memory_space=pltpu.VMEM)
    scratch = [
        pltpu.VMEM((2, H, 2 * H), BF16),
        pltpu.VMEM((2, H, H), BF16),
        pltpu.VMEM((2, H, H), BF16),
        pltpu.VMEM((2, H, 2 * H), BF16),
        pltpu.VMEM((2, 2 * H, H), BF16),
        pltpu.VMEM((2, H, H), BF16),
        pltpu.VMEM((2, 2, H), F32),
    ]
    scratch += [pltpu.VMEM(planes, BF16)] * 4
    scratch += [pltpu.VMEM(planes, F32)] * 4
    scratch += [pltpu.VMEM((2,) + planes, F32)] * 3
    scratch += [pltpu.VMEM(planes, F32)]
    scratch += [pltpu.VMEM((2,) + planes, BF16)] * 3
    scratch += [
        pltpu.VMEM(planes[1:], F32),
        pltpu.VMEM((2,) + planes[1:], F32),
        pltpu.VMEM((2, 2, 16, H), F32),
    ]
    scratch += [pltpu.VMEM((4, 2) + planes[1:], F32)]
    scratch += [pltpu.VMEM((4, 2, 16, 16, H), F32)] * 4
    scratch += [pltpu.VMEM((4, 3, 2, 2, 8, H), F32)] * 2
    scratch += [pltpu.SemaphoreType.DMA((4, 26))] * 2
    n_stage = 2 * (n_x - 1) + 2 * (n_y - 1) + n_z - 1
    for rows in UNITS:
        part_y, part_x = rows // n_y, rows // n_y // n_x
        scratch += [
            pltpu.VMEM((rows, H), F32),
            pltpu.VMEM((n_y - 1, part_y, H), F32),
            pltpu.VMEM((part_y, H), F32),
            pltpu.VMEM((n_x - 1, part_x, H), F32),
            pltpu.VMEM((part_x, H), F32),
            pltpu.VMEM((n_z, part_x, H), F32),
            pltpu.VMEM((part_x, H), F32),
            pltpu.VMEM((part_y, H), F32),
            pltpu.VMEM((rows, H), F32),
        ]
        scratch += [pltpu.SemaphoreType.DMA((n_stage,))] * 2
    outs = pl.pallas_call(
        functools.partial(kernel, sizes, 1.0 / math.sqrt(nodes)),
        out_shape=(
            jax.ShapeDtypeStruct(planes, BF16),
            jax.ShapeDtypeStruct((2, 2, H, H), F32),
            jax.ShapeDtypeStruct((2, 2 * H, H), F32),
            jax.ShapeDtypeStruct((2, H, H), F32),
            jax.ShapeDtypeStruct((2, 2, H), F32),
        ),
        in_specs=[vmem, vmem, pl.BlockSpec(memory_space=pltpu.SMEM), vmem, vmem, vmem, vmem],
        out_specs=(vmem,) * 5,
        scratch_shapes=scratch,
        compiler_params=pltpu.CompilerParams(
            collective_id=0, has_side_effects=True, vmem_limit_bytes=66_000_000
        ),
        name="layers",
    )(
        state.reshape(planes),
        cotangent.reshape(planes),
        counts,
        edge_weights,
        node_in,
        node_out,
        biases,
    )
    return (outs[0].reshape(shape),) + tuple(outs[1:])


def solution(mesh):
    sizes = tuple(mesh.shape[name] for name in AXES)
    grid = P("gx", "gy", "gz", None, None)
    return jax.shard_map(
        functools.partial(on_device, sizes),
        mesh=mesh,
        in_specs=(grid, grid, P("gz"), P(), P(), P(), P()),
        out_specs=(grid, P(), P(), P(), P()),
        check_vma=False,
    )
```

```python
import functools
import math

import jax
import jax.numpy as jnp
from jax import lax
from jax.experimental import pallas as pl
from jax.experimental.pallas import tpu as pltpu
from jax.sharding import PartitionSpec as P

F32 = jnp.float32
BF16 = jnp.bfloat16
H = 128
MESH = pl.DeviceIdType.MESH
AXES = ("gx", "gy", "gz")
UNITS = (512, 512, 256, 256)
GROUPS = ((0, 1), (1, 3), (3, 5), (5, 7), (7, 8))
SIDES = (0, 1)
STARTS = (0, 4, 8, 12)


def mm(a, b):
    return jnp.dot(a, b, preferred_element_type=F32)


def mm_rows(a, b):
    return lax.dot_general(a, b, (((0,), (0,)), ((), ())), preferred_element_type=F32)


def act(x):
    t = jnp.tanh(x)
    m = x * t
    return x + m, (1.0 + t) * ((1.0 + x) - m)


def flat(x):
    return x.reshape(-1, x.shape[-1])


def kernel(sizes, scale, *refs):
    (
        state, cotangent_hbm, counts, edge_w, node_in, node_out, biases,
        state_grad_hbm, grads,
        cotangent, state_grad, load_sem,
        w_first, w_agg, w_out_t, w_in_t, w_two_t, w_one_t, half_bias,
        h_one, g_now, d_now, p_now, pre_a, pre_n, field, dh,
        slope_x, slope_y, slope_z, slope_n, spread, agg, active, inv_yz, carry, bias_acc,
        x_in, rim_out, rim_in, ex_send, ex_recv,
    ) = refs[:42]
    units = [refs[42 + 11 * u : 53 + 11 * u] for u in range(len(UNITS))]
    n_x, n_y, n_z = sizes
    i_x, i_y, i_z = (lax.axis_index(name) for name in AXES)
    here = dict(zip(AXES, (i_x, i_y, i_z)))
    size = dict(zip(AXES, sizes))

    def peer(axis, d):
        return lax.rem(here[axis] + d, size[axis])

    def device(**moves):
        return tuple(peer(a, moves[a] % size[a]) if a in moves else here[a] for a in AXES)

    barrier = pltpu.get_barrier_semaphore()
    partners = [device(**{a: d}) for a in AXES for d in range(1, size[a])]
    partners += [device(gy=dy, gz=dz) for dy in (-1, 1) for dz in (-1, 1)]
    for q in partners:
        pl.semaphore_signal(barrier, inc=1, device_id=q, device_id_type=MESH)
    load = pltpu.make_async_copy(cotangent_hbm, cotangent, load_sem.at[0])
    load.start()

    def flag(cond):
        return jnp.where(cond, 1.0, 0.0).astype(F32)

    live = flag(counts[0] > 1)
    left = {a: flag(here[a] > 0) for a in AXES}
    right = {a: flag(here[a] < size[a] - 1) for a in AXES}

    sk = lax.broadcasted_iota(jnp.int32, (16, H), 0)
    one = jnp.ones((16, H), F32)
    zero = jnp.zeros((16, H), F32)
    row_live = jnp.where(sk < 8, one, one * live)
    not_top = jnp.where((sk == 7) | (sk == 15), zero, one)
    bottom = jnp.where(sk == 0, one, zero)
    top = jnp.where(sk == 7, one * (1.0 - live), jnp.where(sk == 15, one * live, zero))
    bottom_in = bottom * left["gz"]
    top_in = top * right["gz"]
    first_y = bottom * left["gy"]
    last_y = jnp.where(sk == 15, one * right["gy"], zero)
    mult_z = (
        one
        + jnp.where(sk == 0, one * left["gz"], zero)
        + jnp.where(sk == 8, one, zero)
        + jnp.where(sk == 7, one * jnp.maximum(live, right["gz"]), zero)
        + jnp.where(sk == 15, one * right["gz"], zero)
    )
    for y in range(16):
        mult_y = {0: left["gy"], 7: 1.0, 8: 1.0, 15: right["gy"]}.get(y, 0.0)
        inv_yz[y] = 1.0 / (mult_z * (1.0 + mult_y))

    def plane(t, side):
        return 15 - t if side else t

    def inv_x(t, side):
        outer = right["gx"] if side else left["gx"]
        return 1.0 - 0.5 * (flag(t == 0) * outer + flag(t == 7))

    def turn(w):
        return w.astype(F32).T.astype(BF16)

    def half(w):
        return (w.astype(F32) * 0.5).astype(BF16)

    for l in range(2):
        w_first[l] = half(jnp.concatenate([edge_w[l, 0], node_in[l, :H]], 1))
        w_agg[l] = half(node_in[l, H:])
        w_out_t[l] = half(turn(node_out[l]))
        w_in_t[l] = jnp.concatenate([turn(node_in[l, :H]), turn(node_in[l, H:])], 1)
        two_t = half(turn(edge_w[l, 1]))
        w_two_t[l] = jnp.concatenate([two_t, two_t], 0)
        w_one_t[l] = turn(edge_w[l, 0])
    half_bias[...] = biases[...] * 0.5
    for u in units:
        u[0][...] = jnp.zeros_like(u[0])
    bias_acc[...] = jnp.zeros_like(bias_acc)

    at_one = ((3, 0), (1, 0))
    at_two = ((2, 0), (0, 384))
    at_in = ((1, 128), (0, 0))
    at_out = ((1, 384), (0, 256))
    at_bias = (((3, 128), (2, 128)), ((2, 129), (2, 130)))

    def add_grad(place, shift, value):
        u, row = place
        units[u][0][row + shift : row + shift + value.shape[0]] += value

    def steps(order, body, before=None, after=None):
        before, after = before or {}, after or {}

        def step(i, _):
            for k, todo in before.items():
                pl.when(i == k)(todo)
            body(order(i))
            for k, todo in after.items():
                pl.when(i == k)(todo)
            return 0

        lax.fori_loop(0, 8, step, 0)

    def ascending(i):
        return i

    def first_late(i):
        late = lax.div(i, 6)
        return (1 - late) * (i + 1) + late * 7 * (i - 6)

    def first_third(i):
        late = lax.div(i + 5, 8)
        return (1 - late) * lax.rem(i + 1, 3) + late * i

    def roll_k(x, shift):
        n = x.shape[0]
        return pltpu.roll(x.reshape(2 * n, 8, H), shift, 1).reshape(n, 16, H)

    def rows(side, y0):
        return slice(256 * side + 16 * y0, 256 * side + 16 * y0 + 64)

    def cube(x):
        return x.reshape(-1, 16, H)

    def put_first(l, t, h_rows):
        both = mm(h_rows, w_first[l])
        for side in SIDES:
            p = plane(t, side)
            pre_a[p] = cube(both[256 * side : 256 * side + 256, :H])
            pre_n[p] = cube(both[256 * side : 256 * side + 256, H:])

    def put_field(t, chunk):
        k = lax.broadcasted_iota(jnp.int32, (4, 8, H), 1)
        none = jnp.zeros((4, 8, H), F32)
        for side in SIDES:
            p = plane(t, side)
            for y0 in STARTS:
                r = chunk(side, y0)
                low, high = r[:, :8], r[:, 8:] * live
                low2 = low + jnp.where(k == 7, pltpu.roll(high, 7, 1), none)
                high2 = high + jnp.where(k == 0, pltpu.roll(low, 1, 1), none)
                r = jnp.concatenate([low2, high2], 1)
                if y0 == 4:
                    held = r[3:4]
                    field[p, 4:7] = r[:3]
                elif y0 == 8:
                    joint = held + r[0:1]
                    field[p, 7:9] = jnp.concatenate([joint, joint], 0)
                    field[p, 9:12] = r[1:]
                else:
                    field[p, y0 : y0 + 4] = r

    def edge_chunks(t, side, per_edge):
        p = plane(t, side)
        nxt = jnp.maximum(14 - t, 8) if side else jnp.minimum(t + 1, 7)
        zero_row = jnp.zeros((1, 16, H), F32)
        out = []
        for y0 in STARTS:
            ys = slice(y0, y0 + 4)
            mine = pre_a[p, ys]
            if side:
                ux = per_edge(0, pre_a[nxt, ys], mine, p, y0, 4)
                total = ux - carry[side, ys]
            else:
                ux = per_edge(0, mine, pre_a[nxt, ys], p, y0, 4)
                total = carry[side, ys] - ux
            carry[side, ys] = ux
            n = 3 if y0 % 8 else 4
            uy = per_edge(1, mine[:n], pre_a[p, y0 + 1 : y0 + 1 + n], p, y0, n)
            arriving = jnp.concatenate([held if y0 % 8 else zero_row, uy[:3]], 0)
            held = uy[3:4] if n == 4 else None
            leaving = uy if n == 4 else jnp.concatenate([uy, zero_row], 0)
            total = total + (arriving - leaving)
            uz = per_edge(2, mine, roll_k(mine, 7), p, y0, 4)
            total = total + (roll_k(uz, 1) - uz)
            out.append(total.astype(BF16))
        return out

    def remote(src, dst, sem, n, to):
        send, recv = sem
        return pltpu.make_async_remote_copy(
            src_ref=src,
            dst_ref=dst,
            send_sem=send.at[n],
            recv_sem=recv.at[n],
            device_id=to,
            device_id_type=MESH,
        )

    def start(copies):
        for c in copies:
            c.start()

    def wait(src, dst, sem, n):
        whole = remote(src, dst, sem, n, device(gx=1))
        whole.wait_send()
        whole.wait_recv()

    def x_copies(e):
        sem = (ex_send.at[e], ex_recv.at[e])
        n = len(GROUPS)
        return [
            remote(field.at[0], x_in.at[e, 1], sem, n, device(gx=-1)),
            remote(field.at[15], x_in.at[e, 0], sem, n, device(gx=1)),
        ]

    def wait_x(e):
        wait(field.at[pl.ds(0, 2)], x_in.at[e], (ex_send.at[e], ex_recv.at[e]), len(GROUPS))

    def group_copies(e, g):
        sem = (ex_send.at[e], ex_recv.at[e])
        first = 32 if g == 0 else 0
        n = 32 * (GROUPS[g][1] - GROUPS[g][0])

        def one_copy(src, dst, count, to):
            return remote(
                rim_out.at[e, g, pl.ds(src, count)], rim_in.at[e, g, pl.ds(dst, count)], sem, g, to
            )

        copies = []
        for f in (0, 1):
            move = 2 * f - 1
            src, dst = 64 * f + first, 64 * (1 - f) + first
            copies.append(one_copy(src, dst, n, device(gy=move)))
            copies.append(one_copy(128 + src, 128 + dst, n, device(gz=move)))
            for fy in (0, 1):
                src, dst = 256 + 8 * (2 * f + fy), 256 + 8 * (3 - 2 * f - fy)
                copies.append(one_copy(src, dst, 8, device(gy=2 * fy - 1, gz=move)))
        return copies

    def wait_group(e, g):
        n = pl.ds(0, 128 * (GROUPS[g][1] - GROUPS[g][0]) + 32)
        wait(rim_out.at[e, g, n], rim_in.at[e, g, n], (ex_send.at[e], ex_recv.at[e]), g)

    def line(t, side):
        g = lax.div(t + 1, 2)
        return g, 2 * (t + 1 - 2 * g) + side

    def face(kind, f, row):
        return pl.ds(pl.multiple_of(128 * kind + 64 * f + 16 * row, 16), 16)

    def edge_line(f, fy, row):
        return pl.ds(256 + 8 * (2 * f + fy) + row, 1)

    def pack(e, t):
        for side in SIDES:
            p = plane(t, side)
            g, row = line(t, side)
            rim_out[e, g, face(0, 0, row)] = field[p, 0]
            rim_out[e, g, face(0, 1, row)] = field[p, 15]
            for f in (0, 1):
                if f:
                    z = field[p, :, 7, :] * (1.0 - live) + field[p, :, 15, :] * live
                else:
                    z = field[p, :, 0, :]
                rim_out[e, g, face(1, f, row)] = z
                rim_out[e, g, edge_line(f, 0, row)] = z[0:1]
                rim_out[e, g, edge_line(f, 1, row)] = z[15:16]

    def many(*todo):
        def run():
            for one_todo in todo:
                one_todo()

        return run

    def send_x(e):
        return lambda: start(x_copies(e))

    def send(e, g):
        return lambda: start(group_copies(e, g))

    def take(e, g):
        return lambda: wait_group(e, g)

    def outer(e):
        def run():
            wait_x(e)
            field[0] = field[0] + x_in[e, 0] * left["gx"]
            field[15] = field[15] + x_in[e, 1] * right["gx"]
            pack(e, 0)
            start(group_copies(e, 0))

        return run

    def join_middle(e):
        joint = field[7] + field[8]
        field[7] = joint
        field[8] = joint
        pack(e, 7)
        start(group_copies(e, 4))

    def sends(e):
        return {0: send_x(e), 2: send(e, 1), 4: send(e, 2), 6: many(send(e, 3), outer(e))}

    def takes(e):
        return {0: take(e, 1), 2: take(e, 2), 4: take(e, 3), 6: take(e, 0), 7: take(e, 4)}

    def summed(e, t, side):
        p = plane(t, side)
        g, row = line(t, side)
        z = []
        for f in (0, 1):
            z.append(
                rim_in[e, g, face(1, f, row)]
                + rim_in[e, g, edge_line(f, 0, row)] * first_y
                + rim_in[e, g, edge_line(f, 1, row)] * last_y
            )
        out = []
        for y0 in STARTS:
            r = field[p, y0 : y0 + 4]
            if y0 == 0:
                r = jnp.concatenate([r[0:1] + (rim_in[e, g, face(0, 0, row)] * left["gy"])[None], r[1:]], 0)
            if y0 == 12:
                r = jnp.concatenate([r[:3], r[3:4] + (rim_in[e, g, face(0, 1, row)] * right["gy"])[None]], 0)
            r = r + z[0][y0 : y0 + 4][:, None, :] * bottom_in
            out.append(r + z[1][y0 : y0 + 4][:, None, :] * top_in)
        return out

    def messages(l, e):
        carry[...] = jnp.zeros_like(carry)
        bias = half_bias[l, 0:1]
        slopes = (slope_x, slope_y, slope_z)

        def body(t):
            inner = 1.0 - flag(t == 7)

            def per_edge(dim, low, high, p, y0, n):
                u, slope = act((high - low) + bias)
                if dim == 0:
                    u, slope = u * inner, slope * inner
                if dim == 2:
                    u, slope = u * not_top, slope * not_top
                slopes[dim][l, p, y0 : y0 + n] = slope
                return u

            parts = []
            for side in SIDES:
                out = edge_chunks(t, side, per_edge)
                for y0, part in zip(STARTS, out):
                    spread[l, plane(t, side), y0 : y0 + 4] = part
                parts += [flat(part) for part in out]
            r = mm(jnp.concatenate(parts, 0), edge_w[l, 1])
            put_field(t, lambda side, y0: cube(r[rows(side, y0)]))
            pack(e, t)

        steps(ascending, body, after=sends(e))
        join_middle(e)

    def node(l, e, t):
        parts = []
        for side in SIDES:
            p = plane(t, side)
            inv = inv_x(t, side)
            for y0, part in zip(STARTS, summed(e, t, side)):
                a = (part * (inv_yz[y0 : y0 + 4] * inv)).astype(BF16)
                agg[l, p, y0 : y0 + 4] = a
                parts.append(flat(a))
        pre = mm(jnp.concatenate(parts, 0), w_agg[l])
        values, slopes = [], []
        for side in SIDES:
            p = plane(t, side)
            for y0 in STARTS:
                x = pre[rows(side, y0)] + flat(pre_n[p, y0 : y0 + 4]) + half_bias[l, 1:2]
                v, slope = act(x)
                v = v.astype(BF16)
                active[l, p, y0 : y0 + 4] = cube(v)
                values.append(v)
                slopes.append(slope)
        return jnp.concatenate(values, 0), slopes

    def node_back(l, t, g, slopes):
        dv = mm(g, w_out_t[l])
        total = jnp.zeros((16, H), F32)
        parts = []
        for i, slope in enumerate(slopes):
            d = dv[64 * i : 64 * i + 64] * slope
            total = total + jnp.sum(cube(d), 0)
            parts.append(d.astype(BF16))
        bias_acc[l, 1] = bias_acc[l, 1] + total
        d = jnp.concatenate(parts, 0)
        dx = mm(d, w_in_t[l])
        for side in SIDES:
            p = plane(t, side)
            g_now[p] = cube(g[256 * side : 256 * side + 256])
            d_now[p] = cube(d[256 * side : 256 * side + 256])
            for y0 in STARTS:
                at = rows(side, y0)
                dh[p, y0 : y0 + 4] = cube(g[at].astype(F32) + dx[at, :H])
        inv = [inv_x(t, side) for side in SIDES]
        put_field(
            t,
            lambda side, y0: cube(dx[rows(side, y0), H:])
            * (inv_yz[y0 : y0 + 4] * inv[side]),
        )

    def by_fours(body):
        def step(i, _):
            body(pl.ds(4 * i, 4))
            return 0

        lax.fori_loop(0, 4, step, 0)

    def node_grads(l, h_ref):
        def body(at):
            d = flat(d_now[at])
            add_grad(at_out[l], 0, mm_rows(flat(active[l, at]), flat(g_now[at])))
            add_grad(at_in[l], 0, mm_rows(flat(h_ref[at]), d))
            add_grad(at_in[l], H, mm_rows(flat(agg[l, at]), d))

        by_fours(body)

    def first_grad(l, h_ref):
        by_fours(lambda at: add_grad(at_one[l], 0, mm_rows(flat(h_ref[at]), flat(p_now[at]))))

    def edge_first(l, e, after=None):
        def body(t):
            pairs, spreads = [], []
            for side in SIDES:
                spreads.append(flat(spread[l, plane(t, side)]))
                for part in summed(e, t, side):
                    dr = flat(part * row_live)
                    hi = dr.astype(BF16)
                    lo = (dr - hi.astype(F32)).astype(BF16)
                    pairs.append(jnp.concatenate([hi, lo], 1))
            pair = jnp.concatenate(pairs, 0)
            r = mm(pair, w_two_t[l])
            for side in SIDES:
                pre_a[plane(t, side)] = cube(r[256 * side : 256 * side + 256])
            both = mm_rows(jnp.concatenate(spreads, 0), pair)
            add_grad(at_two[l], 0, both[:, :H] + both[:, H:])

        steps(first_late, body, before=takes(e), after=after)

    def edge_back(l, t):
        slopes = (slope_x, slope_y, slope_z)
        sums = []

        def per_edge(dim, low, high, p, y0, n):
            d = (high - low) * slopes[dim][l, p, y0 : y0 + n]
            sums.append(jnp.sum(d, 0))
            return d

        parts = []
        for side in SIDES:
            out = edge_chunks(t, side, per_edge)
            total = functools.reduce(jnp.add, sums)
            sums.clear()
            bias_acc[l, 0] = bias_acc[l, 0] + total
            for y0, part in zip(STARTS, out):
                p_now[plane(t, side), y0 : y0 + 4] = part
            parts += [flat(part) for part in out]
        back = jnp.concatenate(parts, 0)
        held = jnp.concatenate([flat(dh[plane(t, side)]) for side in SIDES], 0)
        return (held + mm(back, w_one_t[l])).astype(BF16), back

    def stage_copies(u, stage):
        (buf, red_y, sum_y, red_x, sum_x, red_z, sum_z, gat_x, gat_y, send_sem, recv_sem) = units[u]
        sem = (send_sem, recv_sem)
        part_y, part_x = UNITS[u] // n_y, UNITS[u] // n_y // n_x

        def part(index, rows):
            return pl.ds(pl.multiple_of(index * rows, 8), rows)

        if stage == 0:
            return [
                remote(buf.at[part(peer("gy", d), part_y)], red_y.at[d - 1], sem, 0, device(gy=d))
                for d in range(1, n_y)
            ]
        if stage == 1:
            return [
                remote(sum_y.at[part(peer("gx", d), part_x)], red_x.at[d - 1], sem, 1, device(gx=d))
                for d in range(1, n_x)
            ]
        if stage == 2:
            return [remote(sum_x, red_z.at[i_z], sem, 2, device(gz=d)) for d in range(1, n_z)]
        if stage == 3:
            return [
                remote(sum_z, gat_x.at[part(i_x, part_x)], sem, 3, device(gx=d))
                for d in range(1, n_x)
            ]
        return [
            remote(gat_x, gat_y.at[part(i_y, part_y)], sem, 4, device(gy=d))
            for d in range(1, n_y)
        ]

    def wait_stage(u, stage):
        (buf, red_y, sum_y, red_x, sum_x, red_z, sum_z, gat_x, gat_y, send_sem, recv_sem) = units[u]
        part_y, part_x = UNITS[u] // n_y, UNITS[u] // n_y // n_x
        most_y, most_x = pl.ds(0, UNITS[u] - part_y), pl.ds(0, part_y - part_x)
        most_z = pl.ds(0, n_z - 1)
        src, dst = (
            (buf.at[most_y], red_y),
            (sum_y.at[most_x], red_x),
            (red_z.at[most_z], red_z.at[most_z]),
            (gat_x.at[most_x], gat_x.at[most_x]),
            (gat_y.at[most_y], gat_y.at[most_y]),
        )[stage]
        wait(src, dst, (send_sem, recv_sem), stage)

    def reduce_step(u, stage):
        (buf, red_y, sum_y, red_x, sum_x, red_z, sum_z, gat_x, gat_y, _, _) = units[u]
        part_y, part_x = UNITS[u] // n_y, UNITS[u] // n_y // n_x
        mine_y = pl.ds(pl.multiple_of(i_y * part_y, 8), part_y)
        mine_x = pl.ds(pl.multiple_of(i_x * part_x, 8), part_x)

        def run():
            if stage > 0:
                wait_stage(u, stage - 1)
            if stage == 1:
                total = buf[mine_y]
                for d in range(1, n_y):
                    total = total + red_y[d - 1]
                sum_y[...] = total
            if stage == 2:
                total = sum_y[mine_x]
                for d in range(1, n_x):
                    total = total + red_x[d - 1]
                sum_x[...] = total
                red_z[i_z] = total
            if stage == 3:
                total = red_z[0]
                for d in range(1, n_z):
                    total = total + red_z[d]
                total = total * scale
                sum_z[...] = total
                gat_x[mine_x] = total
            if stage == 4:
                gat_y[mine_y] = gat_x[...]
            if stage < 5:
                start(stage_copies(u, stage))

        return run

    def finish_bias(l, kind):
        u, row = at_bias[l][kind]
        units[u][0][row : row + 1] = jnp.sum(bias_acc[l, kind], 0, keepdims=True)

    def two(ref, t):
        return jnp.concatenate([flat(ref[plane(t, side)]) for side in SIDES], 0)

    def put_two(ref, t, x):
        for side in SIDES:
            ref[plane(t, side)] = cube(x[256 * side : 256 * side + 256])

    steps(ascending, lambda t: put_first(0, t, two(state, t)))
    pl.semaphore_wait(barrier, len(partners))
    messages(0, 0)

    def middle(t):
        v, slopes = node(0, 0, t)
        put_two(slope_n, t, jnp.concatenate(slopes, 0))
        nxt = (two(state, t).astype(F32) + mm(v, node_out[0])).astype(BF16)
        put_two(h_one, t, nxt)
        put_first(1, t, nxt)

    steps(first_late, middle, before=takes(0))
    messages(1, 1)
    load.wait()

    def last(t):
        _, slopes = node(1, 1, t)
        g = two(cotangent, t)
        g = (cube(g).astype(F32) * row_live).astype(BF16)
        node_back(1, t, flat(g), slopes)
        pack(2, t)

    steps(
        first_third,
        last,
        before={0: take(1, 1), 2: take(1, 0), 3: take(1, 2), 5: take(1, 3), 7: take(1, 4)},
        after={1: send(2, 1), 2: send_x(2), 4: send(2, 2), 6: many(send(2, 3), outer(2))},
    )
    join_middle(2)
    node_grads(1, h_one)
    edge_first(1, 2)
    reduce_step(0, 0)()
    carry[...] = jnp.zeros_like(carry)

    def turnover(t):
        g, _ = edge_back(1, t)
        saved = [slope_n[plane(t, side), y0 : y0 + 4] for side in SIDES for y0 in STARTS]
        node_back(0, t, g, [flat(x) for x in saved])
        pack(3, t)

    after = sends(3)
    after[5] = reduce_step(0, 1)
    steps(ascending, turnover, after=after)
    join_middle(3)
    first_grad(1, h_one)
    node_grads(0, state)
    reduce_step(1, 0)()
    reduce_step(0, 2)()
    finish_bias(0, 1)
    finish_bias(1, 0)
    finish_bias(1, 1)
    edge_first(0, 3)
    reduce_step(2, 0)()
    reduce_step(1, 1)()
    reduce_step(0, 3)()
    carry[...] = jnp.zeros_like(carry)

    def final(t):
        g, back = edge_back(0, t)
        put_two(state_grad, t, g)
        add_grad(at_one[0], 0, mm_rows(two(state, t), back))

    steps(
        ascending,
        final,
        after={6: many(reduce_step(1, 2), reduce_step(0, 4), reduce_step(2, 1))},
    )
    finish_bias(0, 0)
    reduce_step(3, 0)()
    store = pltpu.make_async_copy(state_grad, state_grad_hbm, load_sem.at[1])
    store.start()
    reduce_step(3, 1)()
    reduce_step(1, 3)()
    reduce_step(2, 2)()
    reduce_step(3, 2)()
    reduce_step(0, 5)()
    reduce_step(1, 4)()
    reduce_step(2, 3)()
    reduce_step(3, 3)()
    reduce_step(1, 5)()
    reduce_step(2, 4)()
    reduce_step(2, 5)()
    row = 0
    for u in range(len(UNITS) - 1):
        grads[row : row + UNITS[u]] = units[u][8][...]
        row += UNITS[u]
    store.wait()
    reduce_step(3, 4)()
    reduce_step(3, 5)()
    grads[row : row + UNITS[3]] = units[3][8][...]


def write_out(state_in, grads, state_grad, edge_grads, node_in_grad, node_out_grad, bias_grads):
    state_grad[...] = state_in[...]
    edge_grads[0, 0] = grads[1280:1408]
    edge_grads[0, 1] = grads[1024:1152]
    edge_grads[1, 0] = grads[512:640]
    edge_grads[1, 1] = grads[384:512]
    node_in_grad[0] = grads[640:896]
    node_in_grad[1] = grads[0:256]
    node_out_grad[0] = grads[896:1024]
    node_out_grad[1] = grads[256:384]
    bias_grads[0, 0:1] = grads[1408:1409]
    bias_grads[0, 1:2] = grads[1152:1153]
    bias_grads[1, 0:1] = grads[1153:1154]
    bias_grads[1, 1:2] = grads[1154:1155]


def on_device(sizes, state, cotangent, counts, edge_weights, node_in, node_out, biases):
    n_x, n_y, n_z = sizes
    shape = state.shape
    nodes = (shape[0] * n_x) * (shape[1] * n_y) * (3 * shape[2] * n_z // 4) * shape[3]
    planes = (shape[0], shape[1], shape[2] * shape[3], H)
    vmem = pl.BlockSpec(memory_space=pltpu.VMEM)
    hbm = pl.BlockSpec(memory_space=pl.ANY)
    scratch = [
        pltpu.VMEM(planes, BF16),
        pltpu.VMEM(planes, BF16),
        pltpu.SemaphoreType.DMA((2,)),
        pltpu.VMEM((2, H, 2 * H), BF16),
        pltpu.VMEM((2, H, H), BF16),
        pltpu.VMEM((2, H, H), BF16),
        pltpu.VMEM((2, H, 2 * H), BF16),
        pltpu.VMEM((2, 2 * H, H), BF16),
        pltpu.VMEM((2, H, H), BF16),
        pltpu.VMEM((2, 2, H), F32),
    ]
    scratch += [pltpu.VMEM(planes, BF16)] * 4
    scratch += [pltpu.VMEM(planes, F32)] * 4
    scratch += [pltpu.VMEM((2,) + planes, F32)] * 3
    scratch += [pltpu.VMEM(planes, F32)]
    scratch += [pltpu.VMEM((2,) + planes, BF16)] * 3
    scratch += [
        pltpu.VMEM(planes[1:], F32),
        pltpu.VMEM((2,) + planes[1:], F32),
        pltpu.VMEM((2, 2, 16, H), F32),
    ]
    scratch += [pltpu.VMEM((4, 2) + planes[1:], F32)]
    scratch += [pltpu.VMEM((4, len(GROUPS), 288, H), F32)] * 2
    scratch += [pltpu.SemaphoreType.DMA((4, len(GROUPS) + 1))] * 2
    for rows in UNITS:
        part_y, part_x = rows // n_y, rows // n_y // n_x
        scratch += [
            pltpu.VMEM((rows, H), F32),
            pltpu.VMEM((n_y - 1, part_y, H), F32),
            pltpu.VMEM((part_y, H), F32),
            pltpu.VMEM((n_x - 1, part_x, H), F32),
            pltpu.VMEM((part_x, H), F32),
            pltpu.VMEM((n_z, part_x, H), F32),
            pltpu.VMEM((part_x, H), F32),
            pltpu.VMEM((part_y, H), F32),
            pltpu.VMEM((rows, H), F32),
        ]
        scratch += [pltpu.SemaphoreType.DMA((5,))] * 2
    outs = pl.pallas_call(
        functools.partial(kernel, sizes, 1.0 / math.sqrt(nodes)),
        out_shape=(
            jax.ShapeDtypeStruct(planes, BF16),
            jax.ShapeDtypeStruct((sum(UNITS), H), F32),
        ),
        in_specs=[vmem, hbm, pl.BlockSpec(memory_space=pltpu.SMEM), vmem, vmem, vmem, vmem],
        out_specs=(hbm, vmem),
        scratch_shapes=scratch,
        compiler_params=pltpu.CompilerParams(
            collective_id=0, has_side_effects=True, vmem_limit_bytes=66_000_000
        ),
        name="layers",
    )(
        state.reshape(planes),
        cotangent.reshape(planes),
        counts,
        edge_weights,
        node_in,
        node_out,
        biases,
    )
    outs = pl.pallas_call(
        write_out,
        out_shape=(
            jax.ShapeDtypeStruct(planes, BF16),
            jax.ShapeDtypeStruct((2, 2, H, H), F32),
            jax.ShapeDtypeStruct((2, 2 * H, H), F32),
            jax.ShapeDtypeStruct((2, H, H), F32),
            jax.ShapeDtypeStruct((2, 2, H), F32),
        ),
        in_specs=[vmem, vmem],
        out_specs=(vmem,) * 5,
        name="write_out",
    )(*outs)
    return (outs[0].reshape(shape),) + tuple(outs[1:])


def solution(mesh):
    sizes = tuple(mesh.shape[name] for name in AXES)
    grid = P("gx", "gy", "gz", None, None)
    return jax.shard_map(
        functools.partial(on_device, sizes),
        mesh=mesh,
        in_specs=(grid, grid, P("gz"), P(), P(), P(), P()),
        out_specs=(grid, P(), P(), P(), P()),
        check_vma=False,
    )
```

```python
import functools
import math

import jax
import jax.numpy as jnp
from jax import lax
from jax.experimental import pallas as pl
from jax.experimental.pallas import tpu as pltpu
from jax.sharding import PartitionSpec as P

F32 = jnp.float32
BF16 = jnp.bfloat16
H = 128
MESH = pl.DeviceIdType.MESH
AXES = ("gx", "gy", "gz")
UNITS = (512, 512, 256, 256)
GROUPS = ((0, 1), (1, 3), (3, 5), (5, 7), (7, 8))
SIDES = (0, 1)
STARTS = (0, 4, 8, 12)


def mm(a, b):
    return jnp.dot(a, b, preferred_element_type=F32)


def mm_rows(a, b):
    return lax.dot_general(a, b, (((0,), (0,)), ((), ())), preferred_element_type=F32)


def act(x):
    t = jnp.tanh(x)
    m = x * t
    return x + m, (1.0 + t) * ((1.0 + x) - m)


def flat(x):
    return x.reshape(-1, x.shape[-1])


def kernel(sizes, scale, *refs):
    (
        state, cotangent_hbm, counts, edge_w, node_in, node_out, biases,
        state_grad_hbm, grads,
        cotangent, state_grad, load_sem,
        w_first, w_agg, w_out_t, w_in_t, w_two_t, w_one_t, half_bias,
        h_one, g_now, d_now, p_now, pre_a, pre_n, field, dh,
        slope_x, slope_y, slope_z, slope_n, spread, agg, active, inv_yz, carry, bias_acc,
        x_in, rim_out, rim_in, ex_send, ex_recv,
    ) = refs[:42]
    units = [refs[42 + 11 * u : 53 + 11 * u] for u in range(len(UNITS))]
    n_x, n_y, n_z = sizes
    i_x, i_y, i_z = (lax.axis_index(name) for name in AXES)
    here = dict(zip(AXES, (i_x, i_y, i_z)))
    size = dict(zip(AXES, sizes))

    def peer(axis, d):
        return lax.rem(here[axis] + d, size[axis])

    def device(**moves):
        def place(a):
            if a not in moves:
                return here[a]
            d = moves[a]
            return peer(a, d % size[a] if isinstance(d, int) else d)

        return tuple(place(a) for a in AXES)

    def each(low, high, todo):
        def step(i, _):
            todo(i)
            return 0

        lax.fori_loop(low, high, step, 0)

    barrier = pltpu.get_barrier_semaphore()

    def greet(**moves):
        pl.semaphore_signal(barrier, inc=1, device_id=device(**moves), device_id_type=MESH)

    for a in AXES:
        each(1, size[a], lambda d, a=a: greet(**{a: d}))
    for dy in (-1, 1):
        for dz in (-1, 1):
            greet(gy=dy, gz=dz)
    greeted = n_x + n_y + n_z - 3 + 4
    load = pltpu.make_async_copy(cotangent_hbm, cotangent, load_sem.at[0])
    load.start()

    def flag(cond):
        return jnp.where(cond, 1.0, 0.0).astype(F32)

    live = flag(counts[0] > 1)
    left = {a: flag(here[a] > 0) for a in AXES}
    right = {a: flag(here[a] < size[a] - 1) for a in AXES}

    sk = lax.broadcasted_iota(jnp.int32, (16, H), 0)
    one = jnp.ones((16, H), F32)
    zero = jnp.zeros((16, H), F32)
    row_live = jnp.where(sk < 8, one, one * live)
    not_top = jnp.where((sk == 7) | (sk == 15), zero, one)
    bottom = jnp.where(sk == 0, one, zero)
    top = jnp.where(sk == 7, one * (1.0 - live), jnp.where(sk == 15, one * live, zero))
    bottom_in = bottom * left["gz"]
    top_in = top * right["gz"]
    first_y = bottom * left["gy"]
    last_y = jnp.where(sk == 15, one * right["gy"], zero)
    mult_z = (
        one
        + jnp.where(sk == 0, one * left["gz"], zero)
        + jnp.where(sk == 8, one, zero)
        + jnp.where(sk == 7, one * jnp.maximum(live, right["gz"]), zero)
        + jnp.where(sk == 15, one * right["gz"], zero)
    )
    for y in range(16):
        mult_y = {0: left["gy"], 7: 1.0, 8: 1.0, 15: right["gy"]}.get(y, 0.0)
        inv_yz[y] = 1.0 / (mult_z * (1.0 + mult_y))

    def plane(t, side):
        return 15 - t if side else t

    def inv_x(t, side):
        outer = right["gx"] if side else left["gx"]
        return 1.0 - 0.5 * (flag(t == 0) * outer + flag(t == 7))

    def turn(w):
        return w.astype(F32).T.astype(BF16)

    def half(w):
        return (w.astype(F32) * 0.5).astype(BF16)

    for l in range(2):
        w_first[l] = half(jnp.concatenate([edge_w[l, 0], node_in[l, :H]], 1))
        w_agg[l] = half(node_in[l, H:])
        w_out_t[l] = half(turn(node_out[l]))
        w_in_t[l] = jnp.concatenate([turn(node_in[l, :H]), turn(node_in[l, H:])], 1)
        two_t = half(turn(edge_w[l, 1]))
        w_two_t[l] = jnp.concatenate([two_t, two_t], 0)
        w_one_t[l] = turn(edge_w[l, 0])
    half_bias[...] = biases[...] * 0.5
    for u in units:
        u[0][...] = jnp.zeros_like(u[0])
    bias_acc[...] = jnp.zeros_like(bias_acc)

    at_one = ((3, 0), (1, 0))
    at_two = ((2, 0), (0, 384))
    at_in = ((1, 128), (0, 0))
    at_out = ((1, 384), (0, 256))
    at_bias = (((3, 128), (2, 128)), ((2, 129), (2, 130)))

    def add_grad(place, shift, value):
        u, row = place
        units[u][0][row + shift : row + shift + value.shape[0]] += value

    def steps(order, body, before=None, after=None, groups=None, sent=(2, 4, 6)):
        before, after = before or {}, after or {}

        def step(i, _):
            for k, todo in before.items():
                pl.when(i == k)(todo)
            body(order(i))
            if groups is not None:
                now = functools.reduce(jnp.logical_or, [i == k for k in sent])
                pl.when(now)(lambda: start(group_copies(groups, lax.div(i + 1, 2), 4)))
            for k, todo in after.items():
                pl.when(i == k)(todo)
            return 0

        lax.fori_loop(0, 8, step, 0)

    def ascending(i):
        return i

    def first_late(i):
        late = lax.div(i, 6)
        return (1 - late) * (i + 1) + late * 7 * (i - 6)

    def first_third(i):
        late = lax.div(i + 5, 8)
        return (1 - late) * lax.rem(i + 1, 3) + late * i

    def roll_k(x, shift):
        n = x.shape[0]
        return pltpu.roll(x.reshape(2 * n, 8, H), shift, 1).reshape(n, 16, H)

    def rows(side, y0):
        return slice(256 * side + 16 * y0, 256 * side + 16 * y0 + 64)

    def cube(x):
        return x.reshape(-1, 16, H)

    def put_first(l, t, h_rows):
        both = mm(h_rows, w_first[l])
        for side in SIDES:
            p = plane(t, side)
            pre_a[p] = cube(both[256 * side : 256 * side + 256, :H])
            pre_n[p] = cube(both[256 * side : 256 * side + 256, H:])

    def put_field(t, chunk):
        k = lax.broadcasted_iota(jnp.int32, (4, 8, H), 1)
        none = jnp.zeros((4, 8, H), F32)
        for side in SIDES:
            p = plane(t, side)
            for y0 in STARTS:
                r = chunk(side, y0)
                low, high = r[:, :8], r[:, 8:] * live
                low2 = low + jnp.where(k == 7, pltpu.roll(high, 7, 1), none)
                high2 = high + jnp.where(k == 0, pltpu.roll(low, 1, 1), none)
                r = jnp.concatenate([low2, high2], 1)
                if y0 == 4:
                    held = r[3:4]
                    field[p, 4:7] = r[:3]
                elif y0 == 8:
                    joint = held + r[0:1]
                    field[p, 7:9] = jnp.concatenate([joint, joint], 0)
                    field[p, 9:12] = r[1:]
                else:
                    field[p, y0 : y0 + 4] = r

    def edge_chunks(t, side, per_edge):
        p = plane(t, side)
        nxt = jnp.maximum(14 - t, 8) if side else jnp.minimum(t + 1, 7)
        zero_row = jnp.zeros((1, 16, H), F32)
        out = []
        for y0 in STARTS:
            ys = slice(y0, y0 + 4)
            mine = pre_a[p, ys]
            if side:
                ux = per_edge(0, pre_a[nxt, ys], mine, p, y0, 4)
                total = ux - carry[side, ys]
            else:
                ux = per_edge(0, mine, pre_a[nxt, ys], p, y0, 4)
                total = carry[side, ys] - ux
            carry[side, ys] = ux
            n = 3 if y0 % 8 else 4
            uy = per_edge(1, mine[:n], pre_a[p, y0 + 1 : y0 + 1 + n], p, y0, n)
            arriving = jnp.concatenate([held if y0 % 8 else zero_row, uy[:3]], 0)
            held = uy[3:4] if n == 4 else None
            leaving = uy if n == 4 else jnp.concatenate([uy, zero_row], 0)
            total = total + (arriving - leaving)
            uz = per_edge(2, mine, roll_k(mine, 7), p, y0, 4)
            total = total + (roll_k(uz, 1) - uz)
            out.append(total.astype(BF16))
        return out

    def remote(src, dst, sem, n, to):
        send, recv = sem
        return pltpu.make_async_remote_copy(
            src_ref=src,
            dst_ref=dst,
            send_sem=send.at[n],
            recv_sem=recv.at[n],
            device_id=to,
            device_id_type=MESH,
        )

    def start(copies):
        for c in copies:
            c.start()

    def wait(src, dst, sem, n):
        whole = remote(src, dst, sem, n, device(gx=1))
        whole.wait_send()
        whole.wait_recv()

    def x_copies(e):
        sem = (ex_send.at[e], ex_recv.at[e])
        n = len(GROUPS)
        return [
            remote(field.at[0], x_in.at[e, 1], sem, n, device(gx=-1)),
            remote(field.at[15], x_in.at[e, 0], sem, n, device(gx=1)),
        ]

    def wait_x(e):
        wait(field.at[pl.ds(0, 2)], x_in.at[e], (ex_send.at[e], ex_recv.at[e]), len(GROUPS))

    def group_copies(e, g, planes):
        sem = (ex_send.at[e], ex_recv.at[e])
        first = 0 if planes == 4 or g else 32
        n = 16 * planes

        def one_copy(src, dst, count, to):
            return remote(
                rim_out.at[e, g, pl.ds(src, count)], rim_in.at[e, g, pl.ds(dst, count)], sem, g, to
            )

        copies = []
        for f in (0, 1):
            move = 2 * f - 1
            src, dst = 64 * f + first, 64 * (1 - f) + first
            copies.append(one_copy(src, dst, n, device(gy=move)))
            copies.append(one_copy(128 + src, 128 + dst, n, device(gz=move)))
            for fy in (0, 1):
                src, dst = 256 + 8 * (2 * f + fy), 256 + 8 * (3 - 2 * f - fy)
                copies.append(one_copy(src, dst, 8, device(gy=2 * fy - 1, gz=move)))
        return copies

    def wait_group(e, g):
        n = pl.ds(0, 128 * (GROUPS[g][1] - GROUPS[g][0]) + 32)
        wait(rim_out.at[e, g, n], rim_in.at[e, g, n], (ex_send.at[e], ex_recv.at[e]), g)

    def line(t, side):
        g = lax.div(t + 1, 2)
        return g, 2 * (t + 1 - 2 * g) + side

    def face(kind, f, row):
        return pl.ds(pl.multiple_of(128 * kind + 64 * f + 16 * row, 16), 16)

    def edge_line(f, fy, row):
        return pl.ds(256 + 8 * (2 * f + fy) + row, 1)

    def pack(e, t):
        for side in SIDES:
            p = plane(t, side)
            g, row = line(t, side)
            rim_out[e, g, face(0, 0, row)] = field[p, 0]
            rim_out[e, g, face(0, 1, row)] = field[p, 15]
            for f in (0, 1):
                if f:
                    z = field[p, :, 7, :] * (1.0 - live) + field[p, :, 15, :] * live
                else:
                    z = field[p, :, 0, :]
                rim_out[e, g, face(1, f, row)] = z
                rim_out[e, g, edge_line(f, 0, row)] = z[0:1]
                rim_out[e, g, edge_line(f, 1, row)] = z[15:16]

    def many(*todo):
        def run():
            for one_todo in todo:
                one_todo()

        return run

    def send_x(e):
        return lambda: start(x_copies(e))

    def take(e, g):
        return lambda: wait_group(e, g)

    def outer(e):
        def run():
            wait_x(e)
            field[0] = field[0] + x_in[e, 0] * left["gx"]
            field[15] = field[15] + x_in[e, 1] * right["gx"]
            pack(e, 0)
            start(group_copies(e, 0, 2))

        return run

    def join_middle(e):
        joint = field[7] + field[8]
        field[7] = joint
        field[8] = joint
        pack(e, 7)
        start(group_copies(e, 4, 2))

    def sends(e, *last):
        return {0: send_x(e), 6: many(*last)} if last else {0: send_x(e)}

    def takes(e):
        return {0: take(e, 1), 2: take(e, 2), 4: take(e, 3), 6: take(e, 0), 7: take(e, 4)}

    def summed(e, t, side):
        p = plane(t, side)
        g, row = line(t, side)
        z = []
        for f in (0, 1):
            z.append(
                rim_in[e, g, face(1, f, row)]
                + rim_in[e, g, edge_line(f, 0, row)] * first_y
                + rim_in[e, g, edge_line(f, 1, row)] * last_y
            )
        out = []
        for y0 in STARTS:
            r = field[p, y0 : y0 + 4]
            if y0 == 0:
                r = jnp.concatenate([r[0:1] + (rim_in[e, g, face(0, 0, row)] * left["gy"])[None], r[1:]], 0)
            if y0 == 12:
                r = jnp.concatenate([r[:3], r[3:4] + (rim_in[e, g, face(0, 1, row)] * right["gy"])[None]], 0)
            r = r + z[0][y0 : y0 + 4][:, None, :] * bottom_in
            out.append(r + z[1][y0 : y0 + 4][:, None, :] * top_in)
        return out

    def messages(l, e):
        carry[...] = jnp.zeros_like(carry)
        bias = half_bias[l, 0:1]
        slopes = (slope_x, slope_y, slope_z)

        def body(t):
            inner = 1.0 - flag(t == 7)

            def per_edge(dim, low, high, p, y0, n):
                u, slope = act((high - low) + bias)
                if dim == 0:
                    u, slope = u * inner, slope * inner
                if dim == 2:
                    u, slope = u * not_top, slope * not_top
                slopes[dim][l, p, y0 : y0 + n] = slope
                return u

            parts = []
            for side in SIDES:
                out = edge_chunks(t, side, per_edge)
                for y0, part in zip(STARTS, out):
                    spread[l, plane(t, side), y0 : y0 + 4] = part
                parts += [flat(part) for part in out]
            r = mm(jnp.concatenate(parts, 0), edge_w[l, 1])
            put_field(t, lambda side, y0: cube(r[rows(side, y0)]))
            pack(e, t)

        steps(ascending, body, after=sends(e, outer(e)) if e else sends(e), groups=e)
        join_middle(e)
        if not e:
            outer(e)()

    def node(l, e, t):
        parts = []
        for side in SIDES:
            p = plane(t, side)
            inv = inv_x(t, side)
            for y0, part in zip(STARTS, summed(e, t, side)):
                a = (part * (inv_yz[y0 : y0 + 4] * inv)).astype(BF16)
                agg[l, p, y0 : y0 + 4] = a
                parts.append(flat(a))
        pre = mm(jnp.concatenate(parts, 0), w_agg[l])
        values, slopes = [], []
        for side in SIDES:
            p = plane(t, side)
            for y0 in STARTS:
                x = pre[rows(side, y0)] + flat(pre_n[p, y0 : y0 + 4]) + half_bias[l, 1:2]
                v, slope = act(x)
                v = v.astype(BF16)
                active[l, p, y0 : y0 + 4] = cube(v)
                values.append(v)
                slopes.append(slope)
        return jnp.concatenate(values, 0), slopes

    def node_back(l, t, g, slopes):
        dv = mm(g, w_out_t[l])
        total = jnp.zeros((16, H), F32)
        parts = []
        for i, slope in enumerate(slopes):
            d = dv[64 * i : 64 * i + 64] * slope
            total = total + jnp.sum(cube(d), 0)
            parts.append(d.astype(BF16))
        bias_acc[l, 1] = bias_acc[l, 1] + total
        d = jnp.concatenate(parts, 0)
        dx = mm(d, w_in_t[l])
        for side in SIDES:
            p = plane(t, side)
            g_now[p] = cube(g[256 * side : 256 * side + 256])
            d_now[p] = cube(d[256 * side : 256 * side + 256])
            for y0 in STARTS:
                at = rows(side, y0)
                dh[p, y0 : y0 + 4] = cube(g[at].astype(F32) + dx[at, :H])
        inv = [inv_x(t, side) for side in SIDES]
        put_field(
            t,
            lambda side, y0: cube(dx[rows(side, y0), H:])
            * (inv_yz[y0 : y0 + 4] * inv[side]),
        )

    def by_fours(body, low=0, high=4):
        def step(i, _):
            body(pl.ds(4 * i, 4))
            return 0

        lax.fori_loop(low, high, step, 0)

    def node_grads(l, h_ref, low=0, high=4):
        def body(at):
            d = flat(d_now[at])
            add_grad(at_out[l], 0, mm_rows(flat(active[l, at]), flat(g_now[at])))
            add_grad(at_in[l], 0, mm_rows(flat(h_ref[at]), d))
            add_grad(at_in[l], H, mm_rows(flat(agg[l, at]), d))

        by_fours(body, low, high)

    def first_grad(l, h_ref):
        by_fours(lambda at: add_grad(at_one[l], 0, mm_rows(flat(h_ref[at]), flat(p_now[at]))))

    def edge_first(l, e, after=None):
        def body(t):
            pairs, spreads = [], []
            for side in SIDES:
                spreads.append(flat(spread[l, plane(t, side)]))
                for part in summed(e, t, side):
                    dr = flat(part * row_live)
                    hi = dr.astype(BF16)
                    lo = (dr - hi.astype(F32)).astype(BF16)
                    pairs.append(jnp.concatenate([hi, lo], 1))
            pair = jnp.concatenate(pairs, 0)
            r = mm(pair, w_two_t[l])
            for side in SIDES:
                pre_a[plane(t, side)] = cube(r[256 * side : 256 * side + 256])
            both = mm_rows(jnp.concatenate(spreads, 0), pair)
            add_grad(at_two[l], 0, both[:, :H] + both[:, H:])

        steps(first_late, body, before=takes(e), after=after)

    def edge_back(l, t):
        slopes = (slope_x, slope_y, slope_z)
        sums = []

        def per_edge(dim, low, high, p, y0, n):
            d = (high - low) * slopes[dim][l, p, y0 : y0 + n]
            sums.append(jnp.sum(d, 0))
            return d

        parts = []
        for side in SIDES:
            out = edge_chunks(t, side, per_edge)
            total = functools.reduce(jnp.add, sums)
            sums.clear()
            bias_acc[l, 0] = bias_acc[l, 0] + total
            for y0, part in zip(STARTS, out):
                p_now[plane(t, side), y0 : y0 + 4] = part
            parts += [flat(part) for part in out]
        return jnp.concatenate(parts, 0)

    def state_back(l, t, back):
        held = jnp.concatenate([flat(dh[plane(t, side)]) for side in SIDES], 0)
        return (held + mm(back, w_one_t[l])).astype(BF16)

    def start_stage(u, stage):
        (buf, red_y, sum_y, red_x, sum_x, red_z, sum_z, gat_x, gat_y, send_sem, recv_sem) = units[u]
        sem = (send_sem, recv_sem)
        part_y, part_x = UNITS[u] // n_y, UNITS[u] // n_y // n_x

        def part(index, rows):
            return pl.ds(pl.multiple_of(index * rows, 8), rows)

        def to_z(d):
            remote(sum_x, red_z.at[i_z], sem, stage, device(gz=d)).start()

        def scatter_y(d):
            src = buf.at[part(peer("gy", d), part_y)]
            remote(src, red_y.at[d - 1], sem, 0, device(gy=d)).start()

        def scatter_x(d):
            src = sum_y.at[part(peer("gx", d), part_x)]
            remote(src, red_x.at[d - 1], sem, 1, device(gx=d)).start()

        def gather_x(d):
            remote(sum_z, gat_x.at[part(i_x, part_x)], sem, 3, device(gx=d)).start()

        def gather_y(d):
            remote(gat_x, gat_y.at[part(i_y, part_y)], sem, 4, device(gy=d)).start()

        n, todo = (
            (n_y, scatter_y), (n_x, scatter_x), (n_z, to_z), (n_x, gather_x), (n_y, gather_y)
        )[stage]
        each(1, n, todo)

    def wait_stage(u, stage):
        (buf, red_y, sum_y, red_x, sum_x, red_z, sum_z, gat_x, gat_y, send_sem, recv_sem) = units[u]
        part_y, part_x = UNITS[u] // n_y, UNITS[u] // n_y // n_x
        most_y, most_x = pl.ds(0, UNITS[u] - part_y), pl.ds(0, part_y - part_x)
        most_z = pl.ds(0, n_z - 1)
        src, dst = (
            (buf.at[most_y], red_y),
            (sum_y.at[most_x], red_x),
            (red_z.at[most_z], red_z.at[most_z]),
            (gat_x.at[most_x], gat_x.at[most_x]),
            (gat_y.at[most_y], gat_y.at[most_y]),
        )[stage]
        wait(src, dst, (send_sem, recv_sem), stage)

    def reduce_step(u, stage):
        (buf, red_y, sum_y, red_x, sum_x, red_z, sum_z, gat_x, gat_y, _, _) = units[u]
        part_y, part_x = UNITS[u] // n_y, UNITS[u] // n_y // n_x
        mine_y = pl.ds(pl.multiple_of(i_y * part_y, 8), part_y)
        mine_x = pl.ds(pl.multiple_of(i_x * part_x, 8), part_x)

        def run():
            if stage > 0:
                wait_stage(u, stage - 1)
            if stage == 1:
                total = buf[mine_y]
                for d in range(1, n_y):
                    total = total + red_y[d - 1]
                sum_y[...] = total
            if stage == 2:
                total = sum_y[mine_x]
                for d in range(1, n_x):
                    total = total + red_x[d - 1]
                sum_x[...] = total
                red_z[i_z] = total
            if stage == 3:
                total = red_z[0]
                for d in range(1, n_z):
                    total = total + red_z[d]
                total = total * scale
                sum_z[...] = total
                gat_x[mine_x] = total
            if stage == 4:
                gat_y[mine_y] = gat_x[...]
            if stage < 5:
                start_stage(u, stage)

        return run

    def finish_bias(l, kind):
        u, row = at_bias[l][kind]
        units[u][0][row : row + 1] = jnp.sum(bias_acc[l, kind], 0, keepdims=True)

    def two(ref, t):
        return jnp.concatenate([flat(ref[plane(t, side)]) for side in SIDES], 0)

    def put_two(ref, t, x):
        for side in SIDES:
            ref[plane(t, side)] = cube(x[256 * side : 256 * side + 256])

    steps(ascending, lambda t: put_first(0, t, two(state, t)))
    pl.semaphore_wait(barrier, greeted)
    messages(0, 0)

    def middle(t):
        v, slopes = node(0, 0, t)
        put_two(slope_n, t, jnp.concatenate(slopes, 0))
        nxt = (two(state, t).astype(F32) + mm(v, node_out[0])).astype(BF16)
        put_two(h_one, t, nxt)
        put_first(1, t, nxt)

    steps(first_late, middle, before=takes(0))
    messages(1, 1)
    load.wait()

    def last(t):
        _, slopes = node(1, 1, t)
        g = two(cotangent, t)
        g = (cube(g).astype(F32) * row_live).astype(BF16)
        node_back(1, t, flat(g), slopes)
        pack(2, t)

    steps(
        first_third,
        last,
        before={0: take(1, 1), 2: take(1, 0), 3: take(1, 2), 5: take(1, 3), 7: take(1, 4)},
        after={2: send_x(2)},
        groups=2,
        sent=(1, 4, 6),
    )
    join_middle(2)
    node_grads(1, h_one, 0, 3)
    outer(2)()
    node_grads(1, h_one, 3, 4)
    edge_first(1, 2)
    reduce_step(0, 0)()
    carry[...] = jnp.zeros_like(carry)

    def turnover(t):
        g = state_back(1, t, edge_back(1, t))
        saved = [slope_n[plane(t, side), y0 : y0 + 4] for side in SIDES for y0 in STARTS]
        node_back(0, t, g, [flat(x) for x in saved])
        pack(3, t)

    steps(ascending, turnover, after=sends(3, reduce_step(0, 1)), groups=3)
    join_middle(3)
    outer(3)()
    first_grad(1, h_one)
    node_grads(0, state)
    reduce_step(1, 0)()
    finish_bias(0, 1)
    finish_bias(1, 0)
    finish_bias(1, 1)
    edge_first(0, 3)
    reduce_step(2, 0)()
    reduce_step(0, 2)()
    carry[...] = jnp.zeros_like(carry)

    def final(t):
        back = edge_back(0, t)
        put_two(state_grad, t, state_back(0, t, back))
        add_grad(at_one[0], 0, mm_rows(two(state, t), back))

    steps(ascending, final, after={3: reduce_step(1, 1), 6: reduce_step(2, 1)})
    finish_bias(0, 0)
    reduce_step(3, 0)()
    reduce_step(0, 3)()
    store = pltpu.make_async_copy(state_grad, state_grad_hbm, load_sem.at[1])
    store.start()
    for u, stage in (
        (3, 1), (1, 2), (2, 2), (0, 4), (3, 2), (2, 3), (1, 3), (0, 5), (3, 3), (2, 4), (1, 4),
        (3, 4), (2, 5),
    ):
        reduce_step(u, stage)()
    row = 0
    for u, stage in ((0, None), (1, 5), (2, None), (3, 5)):
        if stage:
            reduce_step(u, stage)()
        grads[row : row + UNITS[u]] = units[u][8][...]
        row += UNITS[u]
    store.wait()


def write_out(state_in, grads, state_grad, edge_grads, node_in_grad, node_out_grad, bias_grads):
    state_grad[...] = state_in[...]
    edge_grads[0, 0] = grads[1280:1408]
    edge_grads[0, 1] = grads[1024:1152]
    edge_grads[1, 0] = grads[512:640]
    edge_grads[1, 1] = grads[384:512]
    node_in_grad[0] = grads[640:896]
    node_in_grad[1] = grads[0:256]
    node_out_grad[0] = grads[896:1024]
    node_out_grad[1] = grads[256:384]
    bias_grads[0, 0:1] = grads[1408:1409]
    bias_grads[0, 1:2] = grads[1152:1153]
    bias_grads[1, 0:1] = grads[1153:1154]
    bias_grads[1, 1:2] = grads[1154:1155]


def on_device(sizes, state, cotangent, counts, edge_weights, node_in, node_out, biases):
    n_x, n_y, n_z = sizes
    shape = state.shape
    nodes = (shape[0] * n_x) * (shape[1] * n_y) * (3 * shape[2] * n_z // 4) * shape[3]
    planes = (shape[0], shape[1], shape[2] * shape[3], H)
    vmem = pl.BlockSpec(memory_space=pltpu.VMEM)
    hbm = pl.BlockSpec(memory_space=pl.ANY)
    scratch = [
        pltpu.VMEM(planes, BF16),
        pltpu.VMEM(planes, BF16),
        pltpu.SemaphoreType.DMA((2,)),
        pltpu.VMEM((2, H, 2 * H), BF16),
        pltpu.VMEM((2, H, H), BF16),
        pltpu.VMEM((2, H, H), BF16),
        pltpu.VMEM((2, H, 2 * H), BF16),
        pltpu.VMEM((2, 2 * H, H), BF16),
        pltpu.VMEM((2, H, H), BF16),
        pltpu.VMEM((2, 2, H), F32),
    ]
    scratch += [pltpu.VMEM(planes, BF16)] * 4
    scratch += [pltpu.VMEM(planes, F32)] * 4
    scratch += [pltpu.VMEM((2,) + planes, F32)] * 3
    scratch += [pltpu.VMEM(planes, F32)]
    scratch += [pltpu.VMEM((2,) + planes, BF16)] * 3
    scratch += [
        pltpu.VMEM(planes[1:], F32),
        pltpu.VMEM((2,) + planes[1:], F32),
        pltpu.VMEM((2, 2, 16, H), F32),
    ]
    scratch += [pltpu.VMEM((4, 2) + planes[1:], F32)]
    scratch += [pltpu.VMEM((4, len(GROUPS), 288, H), F32)] * 2
    scratch += [pltpu.SemaphoreType.DMA((4, len(GROUPS) + 1))] * 2
    for rows in UNITS:
        part_y, part_x = rows // n_y, rows // n_y // n_x
        scratch += [
            pltpu.VMEM((rows, H), F32),
            pltpu.VMEM((n_y - 1, part_y, H), F32),
            pltpu.VMEM((part_y, H), F32),
            pltpu.VMEM((n_x - 1, part_x, H), F32),
            pltpu.VMEM((part_x, H), F32),
            pltpu.VMEM((n_z, part_x, H), F32),
            pltpu.VMEM((part_x, H), F32),
            pltpu.VMEM((part_y, H), F32),
            pltpu.VMEM((rows, H), F32),
        ]
        scratch += [pltpu.SemaphoreType.DMA((5,))] * 2
    outs = pl.pallas_call(
        functools.partial(kernel, sizes, 1.0 / math.sqrt(nodes)),
        out_shape=(
            jax.ShapeDtypeStruct(planes, BF16),
            jax.ShapeDtypeStruct((sum(UNITS), H), F32),
        ),
        in_specs=[vmem, hbm, pl.BlockSpec(memory_space=pltpu.SMEM), vmem, vmem, vmem, vmem],
        out_specs=(hbm, vmem),
        scratch_shapes=scratch,
        compiler_params=pltpu.CompilerParams(
            collective_id=0, has_side_effects=True, vmem_limit_bytes=66_000_000
        ),
        name="layers",
    )(
        state.reshape(planes),
        cotangent.reshape(planes),
        counts,
        edge_weights,
        node_in,
        node_out,
        biases,
    )
    outs = pl.pallas_call(
        write_out,
        out_shape=(
            jax.ShapeDtypeStruct(planes, BF16),
            jax.ShapeDtypeStruct((2, 2, H, H), F32),
            jax.ShapeDtypeStruct((2, 2 * H, H), F32),
            jax.ShapeDtypeStruct((2, H, H), F32),
            jax.ShapeDtypeStruct((2, 2, H), F32),
        ),
        in_specs=[vmem, vmem],
        out_specs=(vmem,) * 5,
        name="write_out",
    )(*outs)
    return (outs[0].reshape(shape),) + tuple(outs[1:])


def solution(mesh):
    sizes = tuple(mesh.shape[name] for name in AXES)
    grid = P("gx", "gy", "gz", None, None)
    return jax.shard_map(
        functools.partial(on_device, sizes),
        mesh=mesh,
        in_specs=(grid, grid, P("gz"), P(), P(), P(), P()),
        out_specs=(grid, P(), P(), P(), P()),
        check_vma=False,
    )
```

```python
import functools
import math

import jax
import jax.numpy as jnp
from jax import lax
from jax.experimental import pallas as pl
from jax.experimental.pallas import tpu as pltpu
from jax.sharding import PartitionSpec as P

F32 = jnp.float32
BF16 = jnp.bfloat16
H = 128
MESH = pl.DeviceIdType.MESH
AXES = ("gx", "gy", "gz")
UNITS = (512, 512, 256, 256)
GROUPS = ((0, 1), (1, 3), (3, 5), (5, 7), (7, 8))
SIDES = (0, 1)
STARTS = (0, 4, 8, 12)


def mm(a, b):
    return jnp.dot(a, b, preferred_element_type=F32)


def mm_rows(a, b):
    return lax.dot_general(a, b, (((0,), (0,)), ((), ())), preferred_element_type=F32)


def act(x):
    t = jnp.tanh(x)
    m = x * t
    return x + m, (1.0 + t) * ((1.0 + x) - m)


def flat(x):
    return x.reshape(-1, x.shape[-1])


def kernel(sizes, scale, *refs):
    (
        state, cotangent_hbm, counts, edge_w, node_in, node_out, biases,
        state_grad_hbm, grads,
        cotangent, state_grad, load_sem,
        w_first, w_agg, w_out_t, w_in_t, w_two_t, w_one_t, half_bias,
        h_one, g_now, d_now, p_now, pre_a, pre_n, field, dh,
        slope_x, slope_y, slope_z, slope_n, spread, agg, active, inv_yz, carry, bias_acc,
        x_in, rim_out, rim_in, ex_send, ex_recv,
    ) = refs[:42]
    units = [refs[42 + 11 * u : 53 + 11 * u] for u in range(len(UNITS))]
    n_x, n_y, n_z = sizes
    i_x, i_y, i_z = (lax.axis_index(name) for name in AXES)
    here = dict(zip(AXES, (i_x, i_y, i_z)))
    size = dict(zip(AXES, sizes))

    def peer(axis, d):
        return lax.rem(here[axis] + d, size[axis])

    def device(**moves):
        def place(a):
            if a not in moves:
                return here[a]
            d = moves[a]
            return peer(a, d % size[a] if isinstance(d, int) else d)

        return tuple(place(a) for a in AXES)

    def each(low, high, todo):
        def step(i, _):
            todo(i)
            return 0

        lax.fori_loop(low, high, step, 0)

    barrier = pltpu.get_barrier_semaphore()

    def greet(**moves):
        pl.semaphore_signal(barrier, inc=1, device_id=device(**moves), device_id_type=MESH)

    for a in AXES:
        each(1, size[a], lambda d, a=a: greet(**{a: d}))
    for dy in (-1, 1):
        for dz in (-1, 1):
            greet(gy=dy, gz=dz)
    greeted = n_x + n_y + n_z - 3 + 4
    load = pltpu.make_async_copy(cotangent_hbm, cotangent, load_sem.at[0])
    load.start()

    def flag(cond):
        return jnp.where(cond, 1.0, 0.0).astype(F32)

    live = flag(counts[0] > 1)
    left = {a: flag(here[a] > 0) for a in AXES}
    right = {a: flag(here[a] < size[a] - 1) for a in AXES}

    sk = lax.broadcasted_iota(jnp.int32, (16, H), 0)
    one = jnp.ones((16, H), F32)
    zero = jnp.zeros((16, H), F32)
    row_live = jnp.where(sk < 8, one, one * live)
    not_top = jnp.where((sk == 7) | (sk == 15), zero, one)
    bottom = jnp.where(sk == 0, one, zero)
    top = jnp.where(sk == 7, one * (1.0 - live), jnp.where(sk == 15, one * live, zero))
    bottom_in = bottom * left["gz"]
    top_in = top * right["gz"]
    first_y = bottom * left["gy"]
    last_y = jnp.where(sk == 15, one * right["gy"], zero)
    mult_z = (
        one
        + jnp.where(sk == 0, one * left["gz"], zero)
        + jnp.where(sk == 8, one, zero)
        + jnp.where(sk == 7, one * jnp.maximum(live, right["gz"]), zero)
        + jnp.where(sk == 15, one * right["gz"], zero)
    )
    for y in range(16):
        mult_y = {0: left["gy"], 7: 1.0, 8: 1.0, 15: right["gy"]}.get(y, 0.0)
        inv_yz[y] = 1.0 / (mult_z * (1.0 + mult_y))

    def plane(t, side):
        return 15 - t if side else t

    def inv_x(t, side):
        outer = right["gx"] if side else left["gx"]
        return 1.0 - 0.5 * (flag(t == 0) * outer + flag(t == 7))

    def turn(w):
        return w.astype(F32).T.astype(BF16)

    def half(w):
        return (w.astype(F32) * 0.5).astype(BF16)

    for l in range(2):
        w_first[l] = half(jnp.concatenate([edge_w[l, 0], node_in[l, :H]], 1))
        w_agg[l] = half(node_in[l, H:])
        w_out_t[l] = half(turn(node_out[l]))
        w_in_t[l] = jnp.concatenate([turn(node_in[l, :H]), turn(node_in[l, H:])], 1)
        two_t = half(turn(edge_w[l, 1]))
        w_two_t[l] = jnp.concatenate([two_t, two_t], 0)
        w_one_t[l] = turn(edge_w[l, 0])
    half_bias[...] = biases[...] * 0.5
    for u in units:
        u[0][...] = jnp.zeros_like(u[0])
    bias_acc[...] = jnp.zeros_like(bias_acc)

    at_one = ((3, 0), (1, 0))
    at_two = ((2, 0), (0, 384))
    at_in = ((1, 128), (0, 0))
    at_out = ((1, 384), (0, 256))
    at_bias = (((3, 128), (2, 128)), ((2, 129), (2, 130)))

    def add_grad(place, shift, value):
        u, row = place
        units[u][0][row + shift : row + shift + value.shape[0]] += value

    def steps(order, body, before=None, after=None, groups=None, sent=(2, 4, 6)):
        before, after = before or {}, after or {}

        def step(i, _):
            for k, todo in before.items():
                pl.when(i == k)(todo)
            body(order(i))
            if groups is not None:
                now = functools.reduce(jnp.logical_or, [i == k for k in sent])
                pl.when(now)(lambda: start(group_copies(groups, lax.div(i + 1, 2), 4)))
            for k, todo in after.items():
                pl.when(i == k)(todo)
            return 0

        lax.fori_loop(0, 8, step, 0)

    def ascending(i):
        return i

    def first_late(i):
        late = lax.div(i, 6)
        return (1 - late) * (i + 1) + late * 7 * (i - 6)

    def first_third(i):
        late = lax.div(i + 5, 8)
        return (1 - late) * lax.rem(i + 1, 3) + late * i

    def roll_k(x, shift):
        n = x.shape[0]
        return pltpu.roll(x.reshape(2 * n, 8, H), shift, 1).reshape(n, 16, H)

    def rows(side, y0):
        return slice(256 * side + 16 * y0, 256 * side + 16 * y0 + 64)

    def cube(x):
        return x.reshape(-1, 16, H)

    def put_first(l, t, h_rows):
        both = mm(h_rows, w_first[l])
        for side in SIDES:
            p = plane(t, side)
            pre_a[p] = cube(both[256 * side : 256 * side + 256, :H])
            pre_n[p] = cube(both[256 * side : 256 * side + 256, H:])

    def put_field(t, chunk):
        k = lax.broadcasted_iota(jnp.int32, (4, 8, H), 1)
        none = jnp.zeros((4, 8, H), F32)
        for side in SIDES:
            p = plane(t, side)
            for y0 in STARTS:
                r = chunk(side, y0)
                low, high = r[:, :8], r[:, 8:] * live
                low2 = low + jnp.where(k == 7, pltpu.roll(high, 7, 1), none)
                high2 = high + jnp.where(k == 0, pltpu.roll(low, 1, 1), none)
                r = jnp.concatenate([low2, high2], 1)
                if y0 == 4:
                    held = r[3:4]
                    field[p, 4:7] = r[:3]
                elif y0 == 8:
                    joint = held + r[0:1]
                    field[p, 7:9] = jnp.concatenate([joint, joint], 0)
                    field[p, 9:12] = r[1:]
                else:
                    field[p, y0 : y0 + 4] = r

    def edge_chunks(t, side, per_edge, bias=None):
        p = plane(t, side)
        nxt = jnp.maximum(14 - t, 8) if side else jnp.minimum(t + 1, 7)
        zero_row = jnp.zeros((1, 16, H), F32)
        out = []
        for y0 in STARTS:
            ys = slice(y0, y0 + 4)
            mine = pre_a[p, ys]
            low = mine if bias is None else mine - bias
            if side:
                high = mine if bias is None else mine + bias
                ux = per_edge(0, pre_a[nxt, ys], high, p, y0, 4)
                total = ux - carry[side, ys]
            else:
                ux = per_edge(0, low, pre_a[nxt, ys], p, y0, 4)
                total = carry[side, ys] - ux
            carry[side, ys] = ux
            n = 3 if y0 % 8 else 4
            uy = per_edge(1, low[:n], pre_a[p, y0 + 1 : y0 + 1 + n], p, y0, n)
            arriving = jnp.concatenate([held if y0 % 8 else zero_row, uy[:3]], 0)
            held = uy[3:4] if n == 4 else None
            leaving = uy if n == 4 else jnp.concatenate([uy, zero_row], 0)
            total = total + (arriving - leaving)
            uz = per_edge(2, low, roll_k(mine, 7), p, y0, 4)
            total = total + (roll_k(uz, 1) - uz)
            out.append(total.astype(BF16))
        return out

    def remote(src, dst, sem, n, to):
        send, recv = sem
        return pltpu.make_async_remote_copy(
            src_ref=src,
            dst_ref=dst,
            send_sem=send.at[n],
            recv_sem=recv.at[n],
            device_id=to,
            device_id_type=MESH,
        )

    def start(copies):
        for c in copies:
            c.start()

    def wait(src, dst, sem, n):
        whole = remote(src, dst, sem, n, device(gx=1))
        whole.wait_send()
        whole.wait_recv()

    def x_copies(e):
        sem = (ex_send.at[e], ex_recv.at[e])
        n = len(GROUPS)
        return [
            remote(field.at[0], x_in.at[e, 1], sem, n, device(gx=-1)),
            remote(field.at[15], x_in.at[e, 0], sem, n, device(gx=1)),
        ]

    def wait_x(e):
        wait(field.at[pl.ds(0, 2)], x_in.at[e], (ex_send.at[e], ex_recv.at[e]), len(GROUPS))

    def group_copies(e, g, planes):
        sem = (ex_send.at[e], ex_recv.at[e])
        first = 0 if planes == 4 or g else 32
        n = 16 * planes

        def one_copy(src, dst, count, to):
            return remote(
                rim_out.at[e, g, pl.ds(src, count)], rim_in.at[e, g, pl.ds(dst, count)], sem, g, to
            )

        copies = []
        for f in (0, 1):
            move = 2 * f - 1
            src, dst = 64 * f + first, 64 * (1 - f) + first
            copies.append(one_copy(src, dst, n, device(gy=move)))
            copies.append(one_copy(128 + src, 128 + dst, n, device(gz=move)))
            for fy in (0, 1):
                src, dst = 256 + 8 * (2 * f + fy), 256 + 8 * (3 - 2 * f - fy)
                copies.append(one_copy(src, dst, 8, device(gy=2 * fy - 1, gz=move)))
        return copies

    def wait_group(e, g):
        n = pl.ds(0, 128 * (GROUPS[g][1] - GROUPS[g][0]) + 32)
        wait(rim_out.at[e, g, n], rim_in.at[e, g, n], (ex_send.at[e], ex_recv.at[e]), g)

    def line(t, side):
        g = lax.div(t + 1, 2)
        return g, 2 * (t + 1 - 2 * g) + side

    def face(kind, f, row):
        return pl.ds(pl.multiple_of(128 * kind + 64 * f + 16 * row, 16), 16)

    def edge_line(f, fy, row):
        return pl.ds(256 + 8 * (2 * f + fy) + row, 1)

    def pack(e, t):
        for side in SIDES:
            p = plane(t, side)
            g, row = line(t, side)
            rim_out[e, g, face(0, 0, row)] = field[p, 0]
            rim_out[e, g, face(0, 1, row)] = field[p, 15]
            for f in (0, 1):
                if f:
                    z = field[p, :, 7, :] * (1.0 - live) + field[p, :, 15, :] * live
                else:
                    z = field[p, :, 0, :]
                rim_out[e, g, face(1, f, row)] = z
                rim_out[e, g, edge_line(f, 0, row)] = z[0:1]
                rim_out[e, g, edge_line(f, 1, row)] = z[15:16]

    def many(*todo):
        def run():
            for one_todo in todo:
                one_todo()

        return run

    def send_x(e):
        return lambda: start(x_copies(e))

    def take(e, g):
        return lambda: wait_group(e, g)

    def outer(e):
        def run():
            wait_x(e)
            field[0] = field[0] + x_in[e, 0] * left["gx"]
            field[15] = field[15] + x_in[e, 1] * right["gx"]
            pack(e, 0)
            start(group_copies(e, 0, 2))

        return run

    def join_middle(e):
        joint = field[7] + field[8]
        field[7] = joint
        field[8] = joint
        pack(e, 7)
        start(group_copies(e, 4, 2))

    def sends(e, *last):
        return {0: send_x(e), 6: many(*last)} if last else {0: send_x(e)}

    def takes(e):
        return {0: take(e, 1), 2: take(e, 2), 4: take(e, 3), 6: take(e, 0), 7: take(e, 4)}

    def summed(e, t, side):
        p = plane(t, side)
        g, row = line(t, side)
        z = []
        for f in (0, 1):
            z.append(
                rim_in[e, g, face(1, f, row)]
                + rim_in[e, g, edge_line(f, 0, row)] * first_y
                + rim_in[e, g, edge_line(f, 1, row)] * last_y
            )
        out = []
        for y0 in STARTS:
            r = field[p, y0 : y0 + 4]
            if y0 == 0:
                r = jnp.concatenate([r[0:1] + (rim_in[e, g, face(0, 0, row)] * left["gy"])[None], r[1:]], 0)
            if y0 == 12:
                r = jnp.concatenate([r[:3], r[3:4] + (rim_in[e, g, face(0, 1, row)] * right["gy"])[None]], 0)
            r = r + z[0][y0 : y0 + 4][:, None, :] * bottom_in
            out.append(r + z[1][y0 : y0 + 4][:, None, :] * top_in)
        return out

    def messages(l, e):
        carry[...] = jnp.zeros_like(carry)
        bias = half_bias[l, 0:1]
        slopes = (slope_x, slope_y, slope_z)

        def body(t):
            inner = 1.0 - flag(t == 7)

            def per_edge(dim, low, high, p, y0, n):
                u, slope = act(high - low)
                if dim == 0:
                    u, slope = u * inner, slope * inner
                if dim == 2:
                    u, slope = u * not_top, slope * not_top
                slopes[dim][l, p, y0 : y0 + n] = slope
                return u

            parts = []
            for side in SIDES:
                out = edge_chunks(t, side, per_edge, bias)
                for y0, part in zip(STARTS, out):
                    spread[l, plane(t, side), y0 : y0 + 4] = part
                parts += [flat(part) for part in out]
            r = mm(jnp.concatenate(parts, 0), edge_w[l, 1])
            put_field(t, lambda side, y0: cube(r[rows(side, y0)]))
            pack(e, t)

        steps(ascending, body, after=sends(e, outer(e)) if e else sends(e), groups=e)
        join_middle(e)
        if not e:
            outer(e)()

    def node(l, e, t):
        parts = []
        for side in SIDES:
            p = plane(t, side)
            inv = inv_x(t, side)
            for y0, part in zip(STARTS, summed(e, t, side)):
                a = (part * (inv_yz[y0 : y0 + 4] * inv)).astype(BF16)
                agg[l, p, y0 : y0 + 4] = a
                parts.append(flat(a))
        pre = mm(jnp.concatenate(parts, 0), w_agg[l])
        values, slopes = [], []
        for side in SIDES:
            p = plane(t, side)
            for y0 in STARTS:
                x = pre[rows(side, y0)] + flat(pre_n[p, y0 : y0 + 4]) + half_bias[l, 1:2]
                v, slope = act(x)
                v = v.astype(BF16)
                active[l, p, y0 : y0 + 4] = cube(v)
                values.append(v)
                slopes.append(slope)
        return jnp.concatenate(values, 0), slopes

    def node_back(l, t, g, slopes):
        dv = mm(g, w_out_t[l])
        total = jnp.zeros((16, H), F32)
        parts = []
        for i, slope in enumerate(slopes):
            d = dv[64 * i : 64 * i + 64] * slope
            total = total + jnp.sum(cube(d), 0)
            parts.append(d.astype(BF16))
        bias_acc[l, 1] = bias_acc[l, 1] + total
        d = jnp.concatenate(parts, 0)
        dx = mm(d, w_in_t[l])
        for side in SIDES:
            p = plane(t, side)
            g_now[p] = cube(g[256 * side : 256 * side + 256])
            d_now[p] = cube(d[256 * side : 256 * side + 256])
            for y0 in STARTS:
                at = rows(side, y0)
                dh[p, y0 : y0 + 4] = cube(g[at].astype(F32) + dx[at, :H])
        inv = [inv_x(t, side) for side in SIDES]
        put_field(
            t,
            lambda side, y0: cube(dx[rows(side, y0), H:])
            * (inv_yz[y0 : y0 + 4] * inv[side]),
        )

    def by_fours(body, low=0, high=4):
        def step(i, _):
            body(pl.ds(4 * i, 4))
            return 0

        lax.fori_loop(low, high, step, 0)

    def node_grads(l, h_ref, low=0, high=4):
        def body(at):
            d = flat(d_now[at])
            add_grad(at_out[l], 0, mm_rows(flat(active[l, at]), flat(g_now[at])))
            add_grad(at_in[l], 0, mm_rows(flat(h_ref[at]), d))
            add_grad(at_in[l], H, mm_rows(flat(agg[l, at]), d))

        by_fours(body, low, high)

    def first_grad(l, h_ref):
        by_fours(lambda at: add_grad(at_one[l], 0, mm_rows(flat(h_ref[at]), flat(p_now[at]))))

    def edge_first(l, e, after=None):
        def body(t):
            pairs, spreads = [], []
            for side in SIDES:
                spreads.append(flat(spread[l, plane(t, side)]))
                for part in summed(e, t, side):
                    dr = flat(part * row_live)
                    hi = dr.astype(BF16)
                    lo = (dr - hi.astype(F32)).astype(BF16)
                    pairs.append(jnp.concatenate([hi, lo], 1))
            pair = jnp.concatenate(pairs, 0)
            r = mm(pair, w_two_t[l])
            for side in SIDES:
                pre_a[plane(t, side)] = cube(r[256 * side : 256 * side + 256])
            both = mm_rows(jnp.concatenate(spreads, 0), pair)
            add_grad(at_two[l], 0, both[:, :H] + both[:, H:])

        steps(first_late, body, before=takes(e), after=after)

    def edge_back(l, t):
        slopes = (slope_x, slope_y, slope_z)
        sums = []

        def per_edge(dim, low, high, p, y0, n):
            d = (high - low) * slopes[dim][l, p, y0 : y0 + n]
            sums.append(jnp.sum(d, 0))
            return d

        parts = []
        for side in SIDES:
            out = edge_chunks(t, side, per_edge)
            total = functools.reduce(jnp.add, sums)
            sums.clear()
            bias_acc[l, 0] = bias_acc[l, 0] + total
            for y0, part in zip(STARTS, out):
                p_now[plane(t, side), y0 : y0 + 4] = part
            parts += [flat(part) for part in out]
        return jnp.concatenate(parts, 0)

    def state_back(l, t, back):
        held = jnp.concatenate([flat(dh[plane(t, side)]) for side in SIDES], 0)
        return (held + mm(back, w_one_t[l])).astype(BF16)

    def start_stage(u, stage):
        (buf, red_y, sum_y, red_x, sum_x, red_z, sum_z, gat_x, gat_y, send_sem, recv_sem) = units[u]
        sem = (send_sem, recv_sem)
        part_y, part_x = UNITS[u] // n_y, UNITS[u] // n_y // n_x

        def part(index, rows):
            return pl.ds(pl.multiple_of(index * rows, 8), rows)

        def to_z(d):
            remote(sum_x, red_z.at[i_z], sem, stage, device(gz=d)).start()

        def scatter_y(d):
            src = buf.at[part(peer("gy", d), part_y)]
            remote(src, red_y.at[d - 1], sem, 0, device(gy=d)).start()

        def scatter_x(d):
            src = sum_y.at[part(peer("gx", d), part_x)]
            remote(src, red_x.at[d - 1], sem, 1, device(gx=d)).start()

        def gather_x(d):
            remote(sum_z, gat_x.at[part(i_x, part_x)], sem, 3, device(gx=d)).start()

        def gather_y(d):
            remote(gat_x, gat_y.at[part(i_y, part_y)], sem, 4, device(gy=d)).start()

        n, todo = (
            (n_y, scatter_y), (n_x, scatter_x), (n_z, to_z), (n_x, gather_x), (n_y, gather_y)
        )[stage]
        each(1, n, todo)

    def wait_stage(u, stage):
        (buf, red_y, sum_y, red_x, sum_x, red_z, sum_z, gat_x, gat_y, send_sem, recv_sem) = units[u]
        part_y, part_x = UNITS[u] // n_y, UNITS[u] // n_y // n_x
        most_y, most_x = pl.ds(0, UNITS[u] - part_y), pl.ds(0, part_y - part_x)
        most_z = pl.ds(0, n_z - 1)
        src, dst = (
            (buf.at[most_y], red_y),
            (sum_y.at[most_x], red_x),
            (red_z.at[most_z], red_z.at[most_z]),
            (gat_x.at[most_x], gat_x.at[most_x]),
            (gat_y.at[most_y], gat_y.at[most_y]),
        )[stage]
        wait(src, dst, (send_sem, recv_sem), stage)

    def reduce_step(u, stage):
        (buf, red_y, sum_y, red_x, sum_x, red_z, sum_z, gat_x, gat_y, _, _) = units[u]
        part_y, part_x = UNITS[u] // n_y, UNITS[u] // n_y // n_x
        mine_y = pl.ds(pl.multiple_of(i_y * part_y, 8), part_y)
        mine_x = pl.ds(pl.multiple_of(i_x * part_x, 8), part_x)

        def run():
            if stage > 0:
                wait_stage(u, stage - 1)
            if stage == 1:
                total = buf[mine_y]
                for d in range(1, n_y):
                    total = total + red_y[d - 1]
                sum_y[...] = total
            if stage == 2:
                total = sum_y[mine_x]
                for d in range(1, n_x):
                    total = total + red_x[d - 1]
                sum_x[...] = total
                red_z[i_z] = total
            if stage == 3:
                total = red_z[0]
                for d in range(1, n_z):
                    total = total + red_z[d]
                total = total * scale
                sum_z[...] = total
                gat_x[mine_x] = total
            if stage == 4:
                gat_y[mine_y] = gat_x[...]
            if stage < 5:
                start_stage(u, stage)

        return run

    def finish_bias(l, kind):
        u, row = at_bias[l][kind]
        units[u][0][row : row + 1] = jnp.sum(bias_acc[l, kind], 0, keepdims=True)

    def two(ref, t):
        return jnp.concatenate([flat(ref[plane(t, side)]) for side in SIDES], 0)

    def put_two(ref, t, x):
        for side in SIDES:
            ref[plane(t, side)] = cube(x[256 * side : 256 * side + 256])

    steps(ascending, lambda t: put_first(0, t, two(state, t)))
    pl.semaphore_wait(barrier, greeted)
    messages(0, 0)

    def middle(t):
        v, slopes = node(0, 0, t)
        put_two(slope_n, t, jnp.concatenate(slopes, 0))
        nxt = (two(state, t).astype(F32) + mm(v, node_out[0])).astype(BF16)
        put_two(h_one, t, nxt)
        put_first(1, t, nxt)

    steps(first_late, middle, before=takes(0))
    messages(1, 1)
    load.wait()

    def last(t):
        _, slopes = node(1, 1, t)
        g = two(cotangent, t)
        g = (cube(g).astype(F32) * row_live).astype(BF16)
        node_back(1, t, flat(g), slopes)
        pack(2, t)

    steps(
        first_third,
        last,
        before={0: take(1, 1), 2: take(1, 0), 3: take(1, 2), 5: take(1, 3), 7: take(1, 4)},
        after={2: send_x(2)},
        groups=2,
        sent=(1, 4, 6),
    )
    join_middle(2)
    node_grads(1, h_one, 0, 3)
    outer(2)()
    node_grads(1, h_one, 3, 4)
    edge_first(1, 2)
    reduce_step(0, 0)()
    carry[...] = jnp.zeros_like(carry)

    def turnover(t):
        g = state_back(1, t, edge_back(1, t))
        saved = [slope_n[plane(t, side), y0 : y0 + 4] for side in SIDES for y0 in STARTS]
        node_back(0, t, g, [flat(x) for x in saved])
        pack(3, t)

    steps(ascending, turnover, after=sends(3), groups=3)
    join_middle(3)
    outer(3)()
    reduce_step(0, 1)()
    first_grad(1, h_one)
    node_grads(0, state)
    reduce_step(1, 0)()
    finish_bias(0, 1)
    finish_bias(1, 0)
    finish_bias(1, 1)
    edge_first(0, 3)
    reduce_step(2, 0)()
    reduce_step(0, 2)()
    carry[...] = jnp.zeros_like(carry)

    def final(t):
        back = edge_back(0, t)
        put_two(state_grad, t, state_back(0, t, back))
        add_grad(at_one[0], 0, mm_rows(two(state, t), back))

    steps(ascending, final, after={5: reduce_step(1, 1)})
    finish_bias(0, 0)
    reduce_step(3, 0)()
    reduce_step(2, 1)()
    reduce_step(0, 3)()
    store = pltpu.make_async_copy(state_grad, state_grad_hbm, load_sem.at[1])
    store.start()
    for u, stage in (
        (3, 1), (1, 2), (2, 2), (0, 4), (3, 2), (2, 3), (1, 3), (0, 5), (3, 3), (2, 4), (1, 4),
        (3, 4), (2, 5),
    ):
        reduce_step(u, stage)()
    row = 0
    for u, stage in ((0, None), (1, 5), (2, None), (3, 5)):
        if stage:
            reduce_step(u, stage)()
        grads[row : row + UNITS[u]] = units[u][8][...]
        row += UNITS[u]
    store.wait()


def write_out(state_in, grads, state_grad, edge_grads, node_in_grad, node_out_grad, bias_grads):
    state_grad[...] = state_in[...]
    edge_grads[0, 0] = grads[1280:1408]
    edge_grads[0, 1] = grads[1024:1152]
    edge_grads[1, 0] = grads[512:640]
    edge_grads[1, 1] = grads[384:512]
    node_in_grad[0] = grads[640:896]
    node_in_grad[1] = grads[0:256]
    node_out_grad[0] = grads[896:1024]
    node_out_grad[1] = grads[256:384]
    bias_grads[0, 0:1] = grads[1408:1409]
    bias_grads[0, 1:2] = grads[1152:1153]
    bias_grads[1, 0:1] = grads[1153:1154]
    bias_grads[1, 1:2] = grads[1154:1155]


def on_device(sizes, state, cotangent, counts, edge_weights, node_in, node_out, biases):
    n_x, n_y, n_z = sizes
    shape = state.shape
    nodes = (shape[0] * n_x) * (shape[1] * n_y) * (3 * shape[2] * n_z // 4) * shape[3]
    planes = (shape[0], shape[1], shape[2] * shape[3], H)
    vmem = pl.BlockSpec(memory_space=pltpu.VMEM)
    hbm = pl.BlockSpec(memory_space=pl.ANY)
    scratch = [
        pltpu.VMEM(planes, BF16),
        pltpu.VMEM(planes, BF16),
        pltpu.SemaphoreType.DMA((2,)),
        pltpu.VMEM((2, H, 2 * H), BF16),
        pltpu.VMEM((2, H, H), BF16),
        pltpu.VMEM((2, H, H), BF16),
        pltpu.VMEM((2, H, 2 * H), BF16),
        pltpu.VMEM((2, 2 * H, H), BF16),
        pltpu.VMEM((2, H, H), BF16),
        pltpu.VMEM((2, 2, H), F32),
    ]
    scratch += [pltpu.VMEM(planes, BF16)] * 4
    scratch += [pltpu.VMEM(planes, F32)] * 4
    scratch += [pltpu.VMEM((2,) + planes, F32)] * 3
    scratch += [pltpu.VMEM(planes, F32)]
    scratch += [pltpu.VMEM((2,) + planes, BF16)] * 3
    scratch += [
        pltpu.VMEM(planes[1:], F32),
        pltpu.VMEM((2,) + planes[1:], F32),
        pltpu.VMEM((2, 2, 16, H), F32),
    ]
    scratch += [pltpu.VMEM((4, 2) + planes[1:], F32)]
    scratch += [pltpu.VMEM((4, len(GROUPS), 288, H), F32)] * 2
    scratch += [pltpu.SemaphoreType.DMA((4, len(GROUPS) + 1))] * 2
    for rows in UNITS:
        part_y, part_x = rows // n_y, rows // n_y // n_x
        scratch += [
            pltpu.VMEM((rows, H), F32),
            pltpu.VMEM((n_y - 1, part_y, H), F32),
            pltpu.VMEM((part_y, H), F32),
            pltpu.VMEM((n_x - 1, part_x, H), F32),
            pltpu.VMEM((part_x, H), F32),
            pltpu.VMEM((n_z, part_x, H), F32),
            pltpu.VMEM((part_x, H), F32),
            pltpu.VMEM((part_y, H), F32),
            pltpu.VMEM((rows, H), F32),
        ]
        scratch += [pltpu.SemaphoreType.DMA((5,))] * 2
    outs = pl.pallas_call(
        functools.partial(kernel, sizes, 1.0 / math.sqrt(nodes)),
        out_shape=(
            jax.ShapeDtypeStruct(planes, BF16),
            jax.ShapeDtypeStruct((sum(UNITS), H), F32),
        ),
        in_specs=[vmem, hbm, pl.BlockSpec(memory_space=pltpu.SMEM), vmem, vmem, vmem, vmem],
        out_specs=(hbm, vmem),
        scratch_shapes=scratch,
        compiler_params=pltpu.CompilerParams(
            collective_id=0, has_side_effects=True, vmem_limit_bytes=66_000_000
        ),
        name="layers",
    )(
        state.reshape(planes),
        cotangent.reshape(planes),
        counts,
        edge_weights,
        node_in,
        node_out,
        biases,
    )
    outs = pl.pallas_call(
        write_out,
        out_shape=(
            jax.ShapeDtypeStruct(planes, BF16),
            jax.ShapeDtypeStruct((2, 2, H, H), F32),
            jax.ShapeDtypeStruct((2, 2 * H, H), F32),
            jax.ShapeDtypeStruct((2, H, H), F32),
            jax.ShapeDtypeStruct((2, 2, H), F32),
        ),
        in_specs=[vmem, vmem],
        out_specs=(vmem,) * 5,
        name="write_out",
    )(*outs)
    return (outs[0].reshape(shape),) + tuple(outs[1:])


def solution(mesh):
    sizes = tuple(mesh.shape[name] for name in AXES)
    grid = P("gx", "gy", "gz", None, None)
    return jax.shard_map(
        functools.partial(on_device, sizes),
        mesh=mesh,
        in_specs=(grid, grid, P("gz"), P(), P(), P(), P()),
        out_specs=(grid, P(), P(), P(), P()),
        check_vma=False,
    )
```

```python
import functools
import math

import jax
import jax.numpy as jnp
from jax import lax
from jax.experimental import pallas as pl
from jax.experimental.pallas import tpu as pltpu
from jax.sharding import PartitionSpec as P

F32 = jnp.float32
BF16 = jnp.bfloat16
H = 128
MESH = pl.DeviceIdType.MESH
AXES = ("gx", "gy", "gz")
UNITS = (512, 512, 256, 256)
GROUPS = ((0, 1), (1, 3), (3, 5), (5, 7), (7, 8))
SIDES = (0, 1)
STARTS = (0, 4, 8, 12)


def mm(a, b):
    return jnp.dot(a, b, preferred_element_type=F32)


def mm_rows(a, b):
    return lax.dot_general(a, b, (((0,), (0,)), ((), ())), preferred_element_type=F32)


def act(x):
    t = jnp.tanh(x)
    m = x * t
    return x + m, (1.0 + t) * ((1.0 + x) - m)


def flat(x):
    return x.reshape(-1, x.shape[-1])


def kernel(sizes, scale, *refs):
    (
        state, cotangent_hbm, counts, edge_w, node_in, node_out, biases,
        state_grad_hbm, grads,
        cotangent, state_grad, load_sem,
        w_first, w_agg, w_out_t, w_in_t, w_two_t, w_one_t, half_bias,
        h_one, g_now, d_now, p_now, pre_a, pre_n, field, dh,
        slope_x, slope_y, slope_z, slope_n, spread, agg, active, inv_yz, carry, bias_acc,
        x_in, rim_out, rim_in, ex_send, ex_recv,
    ) = refs[:42]
    units = [refs[42 + 11 * u : 53 + 11 * u] for u in range(len(UNITS))]
    n_x, n_y, n_z = sizes
    i_x, i_y, i_z = (lax.axis_index(name) for name in AXES)
    here = dict(zip(AXES, (i_x, i_y, i_z)))
    size = dict(zip(AXES, sizes))

    def peer(axis, d):
        return lax.rem(here[axis] + d, size[axis])

    def device(**moves):
        def place(a):
            if a not in moves:
                return here[a]
            d = moves[a]
            return peer(a, d % size[a] if isinstance(d, int) else d)

        return tuple(place(a) for a in AXES)

    def each(low, high, todo):
        def step(i, _):
            todo(i)
            return 0

        lax.fori_loop(low, high, step, 0)

    barrier = pltpu.get_barrier_semaphore()

    def greet(**moves):
        pl.semaphore_signal(barrier, inc=1, device_id=device(**moves), device_id_type=MESH)

    for a in AXES:
        each(1, size[a], lambda d, a=a: greet(**{a: d}))
    for dy in (-1, 1):
        for dz in (-1, 1):
            greet(gy=dy, gz=dz)
    greeted = n_x + n_y + n_z - 3 + 4
    load = pltpu.make_async_copy(cotangent_hbm, cotangent, load_sem.at[0])
    load.start()

    def flag(cond):
        return jnp.where(cond, 1.0, 0.0).astype(F32)

    live = flag(counts[0] > 1)
    left = {a: flag(here[a] > 0) for a in AXES}
    right = {a: flag(here[a] < size[a] - 1) for a in AXES}

    sk = lax.broadcasted_iota(jnp.int32, (16, H), 0)
    one = jnp.ones((16, H), F32)
    zero = jnp.zeros((16, H), F32)
    row_live = jnp.where(sk < 8, one, one * live)
    not_top = jnp.where((sk == 7) | (sk == 15), zero, one)
    bottom = jnp.where(sk == 0, one, zero)
    top = jnp.where(sk == 7, one * (1.0 - live), jnp.where(sk == 15, one * live, zero))
    bottom_in = bottom * left["gz"]
    top_in = top * right["gz"]
    first_y = bottom * left["gy"]
    last_y = jnp.where(sk == 15, one * right["gy"], zero)
    mult_z = (
        one
        + jnp.where(sk == 0, one * left["gz"], zero)
        + jnp.where(sk == 8, one, zero)
        + jnp.where(sk == 7, one * jnp.maximum(live, right["gz"]), zero)
        + jnp.where(sk == 15, one * right["gz"], zero)
    )
    for y in range(16):
        mult_y = {0: left["gy"], 7: 1.0, 8: 1.0, 15: right["gy"]}.get(y, 0.0)
        inv_yz[y] = 1.0 / (mult_z * (1.0 + mult_y))

    def plane(t, side):
        return 15 - t if side else t

    def inv_x(t, side):
        outer = right["gx"] if side else left["gx"]
        return 1.0 - 0.5 * (flag(t == 0) * outer + flag(t == 7))

    def turn(w):
        return w.astype(F32).T.astype(BF16)

    def half(w):
        return (w.astype(F32) * 0.5).astype(BF16)

    for l in range(2):
        w_first[l] = half(jnp.concatenate([edge_w[l, 0], node_in[l, :H]], 1))
        w_agg[l] = half(node_in[l, H:])
        w_out_t[l] = half(turn(node_out[l]))
        w_in_t[l] = jnp.concatenate([turn(node_in[l, :H]), turn(node_in[l, H:])], 1)
        two_t = half(turn(edge_w[l, 1]))
        w_two_t[l] = jnp.concatenate([two_t, two_t], 0)
        w_one_t[l] = turn(edge_w[l, 0])
    half_bias[...] = biases[...] * 0.5
    for u in units:
        u[0][...] = jnp.zeros_like(u[0])
    bias_acc[...] = jnp.zeros_like(bias_acc)

    at_one = ((3, 0), (1, 0))
    at_two = ((2, 0), (0, 384))
    at_in = ((1, 128), (0, 0))
    at_out = ((1, 384), (0, 256))
    at_bias = (((3, 128), (2, 128)), ((2, 129), (2, 130)))

    def add_grad(place, shift, value):
        u, row = place
        units[u][0][row + shift : row + shift + value.shape[0]] += value

    def steps(order, body, before=None, after=None, groups=None, sent=(2, 4, 6)):
        before, after = before or {}, after or {}

        def step(i, _):
            for k, todo in before.items():
                pl.when(i == k)(todo)
            body(order(i))
            if groups is not None:
                now = functools.reduce(jnp.logical_or, [i == k for k in sent])
                pl.when(now)(lambda: start(group_copies(groups, lax.div(i + 1, 2), 4)))
            for k, todo in after.items():
                pl.when(i == k)(todo)
            return 0

        lax.fori_loop(0, 8, step, 0)

    def ascending(i):
        return i

    def first_late(i):
        late = lax.div(i, 6)
        return (1 - late) * (i + 1) + late * 7 * (i - 6)

    def first_third(i):
        late = lax.div(i + 5, 8)
        return (1 - late) * lax.rem(i + 1, 3) + late * i

    def roll_k(x, shift):
        n = x.shape[0]
        return pltpu.roll(x.reshape(2 * n, 8, H), shift, 1).reshape(n, 16, H)

    def rows(side, y0):
        return slice(256 * side + 16 * y0, 256 * side + 16 * y0 + 64)

    def cube(x):
        return x.reshape(-1, 16, H)

    def put_first(l, t, h_rows):
        both = mm(h_rows, w_first[l])
        for side in SIDES:
            p = plane(t, side)
            pre_a[p] = cube(both[256 * side : 256 * side + 256, :H])
            pre_n[p] = cube(both[256 * side : 256 * side + 256, H:])

    def put_field(t, chunk):
        k = lax.broadcasted_iota(jnp.int32, (4, 8, H), 1)
        none = jnp.zeros((4, 8, H), F32)
        for side in SIDES:
            p = plane(t, side)
            for y0 in STARTS:
                r = chunk(side, y0)
                low, high = r[:, :8], r[:, 8:] * live
                low2 = low + jnp.where(k == 7, pltpu.roll(high, 7, 1), none)
                high2 = high + jnp.where(k == 0, pltpu.roll(low, 1, 1), none)
                r = jnp.concatenate([low2, high2], 1)
                if y0 == 4:
                    held = r[3:4]
                    field[p, 4:7] = r[:3]
                elif y0 == 8:
                    joint = held + r[0:1]
                    field[p, 7:9] = jnp.concatenate([joint, joint], 0)
                    field[p, 9:12] = r[1:]
                else:
                    field[p, y0 : y0 + 4] = r

    def edge_chunks(t, side, per_edge, bias=None):
        p = plane(t, side)
        nxt = jnp.maximum(14 - t, 8) if side else jnp.minimum(t + 1, 7)
        zero_row = jnp.zeros((1, 16, H), F32)
        out = []
        for y0 in STARTS:
            ys = slice(y0, y0 + 4)
            mine = pre_a[p, ys]
            low = mine if bias is None else mine - bias
            if side:
                high = mine if bias is None else mine + bias
                ux = per_edge(0, pre_a[nxt, ys], high, p, y0, 4)
                total = ux - carry[side, ys]
            else:
                ux = per_edge(0, low, pre_a[nxt, ys], p, y0, 4)
                total = carry[side, ys] - ux
            carry[side, ys] = ux
            n = 3 if y0 % 8 else 4
            uy = per_edge(1, low[:n], pre_a[p, y0 + 1 : y0 + 1 + n], p, y0, n)
            arriving = jnp.concatenate([held if y0 % 8 else zero_row, uy[:3]], 0)
            held = uy[3:4] if n == 4 else None
            leaving = uy if n == 4 else jnp.concatenate([uy, zero_row], 0)
            total = total + (arriving - leaving)
            uz = per_edge(2, low, roll_k(mine, 7), p, y0, 4)
            total = total + (roll_k(uz, 1) - uz)
            out.append(total.astype(BF16))
        return out

    def remote(src, dst, sem, n, to):
        send, recv = sem
        return pltpu.make_async_remote_copy(
            src_ref=src,
            dst_ref=dst,
            send_sem=send.at[n],
            recv_sem=recv.at[n],
            device_id=to,
            device_id_type=MESH,
        )

    def start(copies):
        for c in copies:
            c.start()

    def wait(src, dst, sem, n):
        whole = remote(src, dst, sem, n, device(gx=1))
        whole.wait_send()
        whole.wait_recv()

    def x_copies(e):
        sem = (ex_send.at[e], ex_recv.at[e])
        n = len(GROUPS)
        return [
            remote(field.at[0], x_in.at[e, 1], sem, n, device(gx=-1)),
            remote(field.at[15], x_in.at[e, 0], sem, n, device(gx=1)),
        ]

    def wait_x(e):
        wait(field.at[pl.ds(0, 2)], x_in.at[e], (ex_send.at[e], ex_recv.at[e]), len(GROUPS))

    def group_copies(e, g, planes):
        sem = (ex_send.at[e], ex_recv.at[e])
        first = 0 if planes == 4 or g else 32
        n = 16 * planes

        def one_copy(src, dst, count, to):
            return remote(
                rim_out.at[e, g, pl.ds(src, count)], rim_in.at[e, g, pl.ds(dst, count)], sem, g, to
            )

        copies = []
        for f in (0, 1):
            move = 2 * f - 1
            src, dst = 64 * f + first, 64 * (1 - f) + first
            copies.insert(f, one_copy(128 + src, 128 + dst, n, device(gz=move)))
            copies.append(one_copy(src, dst, n, device(gy=move)))
            for fy in (0, 1):
                src, dst = 256 + 8 * (2 * f + fy), 256 + 8 * (3 - 2 * f - fy)
                copies.append(one_copy(src, dst, 8, device(gy=2 * fy - 1, gz=move)))
        return copies

    def wait_group(e, g):
        n = pl.ds(0, 128 * (GROUPS[g][1] - GROUPS[g][0]) + 32)
        wait(rim_out.at[e, g, n], rim_in.at[e, g, n], (ex_send.at[e], ex_recv.at[e]), g)

    def line(t, side):
        g = lax.div(t + 1, 2)
        return g, 2 * (t + 1 - 2 * g) + side

    def face(kind, f, row):
        return pl.ds(pl.multiple_of(128 * kind + 64 * f + 16 * row, 16), 16)

    def edge_line(f, fy, row):
        return pl.ds(256 + 8 * (2 * f + fy) + row, 1)

    def pack(e, t):
        for side in SIDES:
            p = plane(t, side)
            g, row = line(t, side)
            rim_out[e, g, face(0, 0, row)] = field[p, 0]
            rim_out[e, g, face(0, 1, row)] = field[p, 15]
            for f in (0, 1):
                if f:
                    z = field[p, :, 7, :] * (1.0 - live) + field[p, :, 15, :] * live
                else:
                    z = field[p, :, 0, :]
                rim_out[e, g, face(1, f, row)] = z
                rim_out[e, g, edge_line(f, 0, row)] = z[0:1]
                rim_out[e, g, edge_line(f, 1, row)] = z[15:16]

    def many(*todo):
        def run():
            for one_todo in todo:
                one_todo()

        return run

    def send_x(e):
        return lambda: start(x_copies(e))

    def take(e, g):
        return lambda: wait_group(e, g)

    def outer(e):
        def run():
            wait_x(e)
            field[0] = field[0] + x_in[e, 0] * left["gx"]
            field[15] = field[15] + x_in[e, 1] * right["gx"]
            pack(e, 0)
            start(group_copies(e, 0, 2))

        return run

    def join_middle(e):
        joint = field[7] + field[8]
        field[7] = joint
        field[8] = joint
        pack(e, 7)
        start(group_copies(e, 4, 2))

    def sends(e, *last):
        return {0: send_x(e), 6: many(*last)} if last else {0: send_x(e)}

    def takes(e):
        return {0: take(e, 1), 2: take(e, 2), 4: take(e, 3), 6: take(e, 0), 7: take(e, 4)}

    def summed(e, t, side):
        p = plane(t, side)
        g, row = line(t, side)
        z = []
        for f in (0, 1):
            z.append(
                rim_in[e, g, face(1, f, row)]
                + rim_in[e, g, edge_line(f, 0, row)] * first_y
                + rim_in[e, g, edge_line(f, 1, row)] * last_y
            )
        out = []
        for y0 in STARTS:
            r = field[p, y0 : y0 + 4]
            if y0 == 0:
                r = jnp.concatenate([r[0:1] + (rim_in[e, g, face(0, 0, row)] * left["gy"])[None], r[1:]], 0)
            if y0 == 12:
                r = jnp.concatenate([r[:3], r[3:4] + (rim_in[e, g, face(0, 1, row)] * right["gy"])[None]], 0)
            r = r + z[0][y0 : y0 + 4][:, None, :] * bottom_in
            out.append(r + z[1][y0 : y0 + 4][:, None, :] * top_in)
        return out

    def messages(l, e):
        carry[...] = jnp.zeros_like(carry)
        bias = half_bias[l, 0:1]
        slopes = (slope_x, slope_y, slope_z)

        def body(t):
            inner = 1.0 - flag(t == 7)

            def per_edge(dim, low, high, p, y0, n):
                u, slope = act(high - low)
                if dim == 0:
                    u, slope = u * inner, slope * inner
                if dim == 2:
                    u, slope = u * not_top, slope * not_top
                slopes[dim][l, p, y0 : y0 + n] = slope
                return u

            parts = []
            for side in SIDES:
                out = edge_chunks(t, side, per_edge, bias)
                for y0, part in zip(STARTS, out):
                    spread[l, plane(t, side), y0 : y0 + 4] = part
                parts += [flat(part) for part in out]
            r = mm(jnp.concatenate(parts, 0), edge_w[l, 1])
            put_field(t, lambda side, y0: cube(r[rows(side, y0)]))
            pack(e, t)

        steps(ascending, body, after=sends(e, outer(e)) if e else sends(e), groups=e)
        join_middle(e)
        if not e:
            outer(e)()

    def node(l, e, t):
        parts = []
        for side in SIDES:
            p = plane(t, side)
            inv = inv_x(t, side)
            for y0, part in zip(STARTS, summed(e, t, side)):
                a = (part * (inv_yz[y0 : y0 + 4] * inv)).astype(BF16)
                agg[l, p, y0 : y0 + 4] = a
                parts.append(flat(a))
        pre = mm(jnp.concatenate(parts, 0), w_agg[l])
        values, slopes = [], []
        for side in SIDES:
            p = plane(t, side)
            for y0 in STARTS:
                x = pre[rows(side, y0)] + flat(pre_n[p, y0 : y0 + 4]) + half_bias[l, 1:2]
                v, slope = act(x)
                v = v.astype(BF16)
                active[l, p, y0 : y0 + 4] = cube(v)
                values.append(v)
                slopes.append(slope)
        return jnp.concatenate(values, 0), slopes

    def node_back(l, t, g, slopes):
        dv = mm(g, w_out_t[l])
        total = jnp.zeros((16, H), F32)
        parts = []
        for i, slope in enumerate(slopes):
            d = dv[64 * i : 64 * i + 64] * slope
            total = total + jnp.sum(cube(d), 0)
            parts.append(d.astype(BF16))
        bias_acc[l, 1] = bias_acc[l, 1] + total
        d = jnp.concatenate(parts, 0)
        dx = mm(d, w_in_t[l])
        for side in SIDES:
            p = plane(t, side)
            g_now[p] = cube(g[256 * side : 256 * side + 256])
            d_now[p] = cube(d[256 * side : 256 * side + 256])
            for y0 in STARTS:
                at = rows(side, y0)
                dh[p, y0 : y0 + 4] = cube(g[at].astype(F32) + dx[at, :H])
        inv = [inv_x(t, side) for side in SIDES]
        put_field(
            t,
            lambda side, y0: cube(dx[rows(side, y0), H:])
            * (inv_yz[y0 : y0 + 4] * inv[side]),
        )

    def by_fours(body, low=0, high=4):
        def step(i, _):
            body(pl.ds(4 * i, 4))
            return 0

        lax.fori_loop(low, high, step, 0)

    def node_grads(l, h_ref, low=0, high=4):
        def body(at):
            d = flat(d_now[at])
            add_grad(at_out[l], 0, mm_rows(flat(active[l, at]), flat(g_now[at])))
            add_grad(at_in[l], 0, mm_rows(flat(h_ref[at]), d))
            add_grad(at_in[l], H, mm_rows(flat(agg[l, at]), d))

        by_fours(body, low, high)

    def first_grad(l, h_ref):
        by_fours(lambda at: add_grad(at_one[l], 0, mm_rows(flat(h_ref[at]), flat(p_now[at]))))

    def edge_first(l, e, after=None):
        def body(t):
            pairs, spreads = [], []
            for side in SIDES:
                spreads.append(flat(spread[l, plane(t, side)]))
                for part in summed(e, t, side):
                    dr = flat(part * row_live)
                    hi = dr.astype(BF16)
                    lo = (dr - hi.astype(F32)).astype(BF16)
                    pairs.append(jnp.concatenate([hi, lo], 1))
            pair = jnp.concatenate(pairs, 0)
            r = mm(pair, w_two_t[l])
            for side in SIDES:
                pre_a[plane(t, side)] = cube(r[256 * side : 256 * side + 256])
            both = mm_rows(jnp.concatenate(spreads, 0), pair)
            add_grad(at_two[l], 0, both[:, :H] + both[:, H:])

        steps(first_late, body, before=takes(e), after=after)

    def edge_back(l, t):
        slopes = (slope_x, slope_y, slope_z)
        sums = []

        def per_edge(dim, low, high, p, y0, n):
            d = (high - low) * slopes[dim][l, p, y0 : y0 + n]
            sums.append(jnp.sum(d, 0))
            return d

        parts = []
        for side in SIDES:
            out = edge_chunks(t, side, per_edge)
            total = functools.reduce(jnp.add, sums)
            sums.clear()
            bias_acc[l, 0] = bias_acc[l, 0] + total
            for y0, part in zip(STARTS, out):
                p_now[plane(t, side), y0 : y0 + 4] = part
            parts += [flat(part) for part in out]
        return jnp.concatenate(parts, 0)

    def state_back(l, t, back):
        held = jnp.concatenate([flat(dh[plane(t, side)]) for side in SIDES], 0)
        return (held + mm(back, w_one_t[l])).astype(BF16)

    def start_stage(u, stage):
        (buf, red_y, sum_y, red_x, sum_x, red_z, sum_z, gat_x, gat_y, send_sem, recv_sem) = units[u]
        sem = (send_sem, recv_sem)
        part_y, part_x = UNITS[u] // n_y, UNITS[u] // n_y // n_x

        def part(index, rows):
            return pl.ds(pl.multiple_of(index * rows, 8), rows)

        def to_z(d):
            remote(sum_x, red_z.at[i_z], sem, stage, device(gz=d)).start()

        def scatter_y(d):
            src = buf.at[part(peer("gy", d), part_y)]
            remote(src, red_y.at[d - 1], sem, 0, device(gy=d)).start()

        def scatter_x(d):
            src = sum_y.at[part(peer("gx", d), part_x)]
            remote(src, red_x.at[d - 1], sem, 1, device(gx=d)).start()

        def gather_x(d):
            remote(sum_z, gat_x.at[part(i_x, part_x)], sem, 3, device(gx=d)).start()

        def gather_y(d):
            remote(gat_x, gat_y.at[part(i_y, part_y)], sem, 4, device(gy=d)).start()

        n, todo = (
            (n_y, scatter_y), (n_x, scatter_x), (n_z, to_z), (n_x, gather_x), (n_y, gather_y)
        )[stage]
        each(1, n, todo)

    def wait_stage(u, stage):
        (buf, red_y, sum_y, red_x, sum_x, red_z, sum_z, gat_x, gat_y, send_sem, recv_sem) = units[u]
        part_y, part_x = UNITS[u] // n_y, UNITS[u] // n_y // n_x
        most_y, most_x = pl.ds(0, UNITS[u] - part_y), pl.ds(0, part_y - part_x)
        most_z = pl.ds(0, n_z - 1)
        src, dst = (
            (buf.at[most_y], red_y),
            (sum_y.at[most_x], red_x),
            (red_z.at[most_z], red_z.at[most_z]),
            (gat_x.at[most_x], gat_x.at[most_x]),
            (gat_y.at[most_y], gat_y.at[most_y]),
        )[stage]
        wait(src, dst, (send_sem, recv_sem), stage)

    def reduce_step(u, stage):
        (buf, red_y, sum_y, red_x, sum_x, red_z, sum_z, gat_x, gat_y, _, _) = units[u]
        part_y, part_x = UNITS[u] // n_y, UNITS[u] // n_y // n_x
        mine_y = pl.ds(pl.multiple_of(i_y * part_y, 8), part_y)
        mine_x = pl.ds(pl.multiple_of(i_x * part_x, 8), part_x)

        def run():
            if stage > 0:
                wait_stage(u, stage - 1)
            if stage == 1:
                total = buf[mine_y]
                for d in range(1, n_y):
                    total = total + red_y[d - 1]
                sum_y[...] = total
            if stage == 2:
                total = sum_y[mine_x]
                for d in range(1, n_x):
                    total = total + red_x[d - 1]
                sum_x[...] = total
                red_z[i_z] = total
            if stage == 3:
                total = red_z[0]
                for d in range(1, n_z):
                    total = total + red_z[d]
                total = total * scale
                sum_z[...] = total
                gat_x[mine_x] = total
            if stage == 4:
                gat_y[mine_y] = gat_x[...]
            if stage < 5:
                start_stage(u, stage)

        return run

    def finish_bias(l, kind):
        u, row = at_bias[l][kind]
        units[u][0][row : row + 1] = jnp.sum(bias_acc[l, kind], 0, keepdims=True)

    def two(ref, t):
        return jnp.concatenate([flat(ref[plane(t, side)]) for side in SIDES], 0)

    def put_two(ref, t, x):
        for side in SIDES:
            ref[plane(t, side)] = cube(x[256 * side : 256 * side + 256])

    steps(ascending, lambda t: put_first(0, t, two(state, t)))
    pl.semaphore_wait(barrier, greeted)
    messages(0, 0)

    def middle(t):
        v, slopes = node(0, 0, t)
        put_two(slope_n, t, jnp.concatenate(slopes, 0))
        nxt = (two(state, t).astype(F32) + mm(v, node_out[0])).astype(BF16)
        put_two(h_one, t, nxt)
        put_first(1, t, nxt)

    steps(first_late, middle, before=takes(0))
    messages(1, 1)
    load.wait()

    def last(t):
        _, slopes = node(1, 1, t)
        g = two(cotangent, t)
        g = (cube(g).astype(F32) * row_live).astype(BF16)
        node_back(1, t, flat(g), slopes)
        pack(2, t)

    steps(
        first_third,
        last,
        before={0: take(1, 1), 2: take(1, 0), 3: take(1, 2), 5: take(1, 3), 7: take(1, 4)},
        after={2: send_x(2)},
        groups=2,
        sent=(1, 4, 6),
    )
    join_middle(2)
    node_grads(1, h_one, 0, 3)
    outer(2)()
    node_grads(1, h_one, 3, 4)
    edge_first(1, 2)
    reduce_step(0, 0)()
    carry[...] = jnp.zeros_like(carry)

    def turnover(t):
        g = state_back(1, t, edge_back(1, t))
        saved = [slope_n[plane(t, side), y0 : y0 + 4] for side in SIDES for y0 in STARTS]
        node_back(0, t, g, [flat(x) for x in saved])
        pack(3, t)

    steps(ascending, turnover, after=sends(3), groups=3)
    join_middle(3)
    outer(3)()
    reduce_step(0, 1)()
    first_grad(1, h_one)
    node_grads(0, state)
    reduce_step(1, 0)()
    finish_bias(0, 1)
    finish_bias(1, 0)
    finish_bias(1, 1)
    edge_first(0, 3)
    reduce_step(2, 0)()
    reduce_step(0, 2)()
    carry[...] = jnp.zeros_like(carry)

    def final(t):
        back = edge_back(0, t)
        put_two(state_grad, t, state_back(0, t, back))
        add_grad(at_one[0], 0, mm_rows(two(state, t), back))

    steps(ascending, final, after={5: reduce_step(1, 1)})
    finish_bias(0, 0)
    reduce_step(3, 0)()
    reduce_step(2, 1)()
    reduce_step(0, 3)()
    store = pltpu.make_async_copy(state_grad, state_grad_hbm, load_sem.at[1])
    store.start()
    for u, stage in (
        (3, 1), (1, 2), (2, 2), (0, 4), (3, 2), (2, 3), (1, 3), (0, 5), (3, 3), (2, 4), (1, 4),
        (3, 4), (2, 5),
    ):
        reduce_step(u, stage)()
    row = 0
    for u, stage in ((0, None), (1, 5), (2, None), (3, 5)):
        if stage:
            reduce_step(u, stage)()
        grads[row : row + UNITS[u]] = units[u][8][...]
        row += UNITS[u]
    store.wait()


def write_out(state_in, grads, state_grad, edge_grads, node_in_grad, node_out_grad, bias_grads):
    state_grad[...] = state_in[...]
    edge_grads[0, 0] = grads[1280:1408]
    edge_grads[0, 1] = grads[1024:1152]
    edge_grads[1, 0] = grads[512:640]
    edge_grads[1, 1] = grads[384:512]
    node_in_grad[0] = grads[640:896]
    node_in_grad[1] = grads[0:256]
    node_out_grad[0] = grads[896:1024]
    node_out_grad[1] = grads[256:384]
    bias_grads[0, 0:1] = grads[1408:1409]
    bias_grads[0, 1:2] = grads[1152:1153]
    bias_grads[1, 0:1] = grads[1153:1154]
    bias_grads[1, 1:2] = grads[1154:1155]


def on_device(sizes, state, cotangent, counts, edge_weights, node_in, node_out, biases):
    n_x, n_y, n_z = sizes
    shape = state.shape
    nodes = (shape[0] * n_x) * (shape[1] * n_y) * (3 * shape[2] * n_z // 4) * shape[3]
    planes = (shape[0], shape[1], shape[2] * shape[3], H)
    vmem = pl.BlockSpec(memory_space=pltpu.VMEM)
    hbm = pl.BlockSpec(memory_space=pl.ANY)
    scratch = [
        pltpu.VMEM(planes, BF16),
        pltpu.VMEM(planes, BF16),
        pltpu.SemaphoreType.DMA((2,)),
        pltpu.VMEM((2, H, 2 * H), BF16),
        pltpu.VMEM((2, H, H), BF16),
        pltpu.VMEM((2, H, H), BF16),
        pltpu.VMEM((2, H, 2 * H), BF16),
        pltpu.VMEM((2, 2 * H, H), BF16),
        pltpu.VMEM((2, H, H), BF16),
        pltpu.VMEM((2, 2, H), F32),
    ]
    scratch += [pltpu.VMEM(planes, BF16)] * 4
    scratch += [pltpu.VMEM(planes, F32)] * 4
    scratch += [pltpu.VMEM((2,) + planes, F32)] * 3
    scratch += [pltpu.VMEM(planes, F32)]
    scratch += [pltpu.VMEM((2,) + planes, BF16)] * 3
    scratch += [
        pltpu.VMEM(planes[1:], F32),
        pltpu.VMEM((2,) + planes[1:], F32),
        pltpu.VMEM((2, 2, 16, H), F32),
    ]
    scratch += [pltpu.VMEM((4, 2) + planes[1:], F32)]
    scratch += [pltpu.VMEM((4, len(GROUPS), 288, H), F32)] * 2
    scratch += [pltpu.SemaphoreType.DMA((4, len(GROUPS) + 1))] * 2
    for rows in UNITS:
        part_y, part_x = rows // n_y, rows // n_y // n_x
        scratch += [
            pltpu.VMEM((rows, H), F32),
            pltpu.VMEM((n_y - 1, part_y, H), F32),
            pltpu.VMEM((part_y, H), F32),
            pltpu.VMEM((n_x - 1, part_x, H), F32),
            pltpu.VMEM((part_x, H), F32),
            pltpu.VMEM((n_z, part_x, H), F32),
            pltpu.VMEM((part_x, H), F32),
            pltpu.VMEM((part_y, H), F32),
            pltpu.VMEM((rows, H), F32),
        ]
        scratch += [pltpu.SemaphoreType.DMA((5,))] * 2
    outs = pl.pallas_call(
        functools.partial(kernel, sizes, 1.0 / math.sqrt(nodes)),
        out_shape=(
            jax.ShapeDtypeStruct(planes, BF16),
            jax.ShapeDtypeStruct((sum(UNITS), H), F32),
        ),
        in_specs=[vmem, hbm, pl.BlockSpec(memory_space=pltpu.SMEM), vmem, vmem, vmem, vmem],
        out_specs=(hbm, vmem),
        scratch_shapes=scratch,
        compiler_params=pltpu.CompilerParams(
            collective_id=0, has_side_effects=True, vmem_limit_bytes=66_000_000
        ),
        name="layers",
    )(
        state.reshape(planes),
        cotangent.reshape(planes),
        counts,
        edge_weights,
        node_in,
        node_out,
        biases,
    )
    outs = pl.pallas_call(
        write_out,
        out_shape=(
            jax.ShapeDtypeStruct(planes, BF16),
            jax.ShapeDtypeStruct((2, 2, H, H), F32),
            jax.ShapeDtypeStruct((2, 2 * H, H), F32),
            jax.ShapeDtypeStruct((2, H, H), F32),
            jax.ShapeDtypeStruct((2, 2, H), F32),
        ),
        in_specs=[vmem, vmem],
        out_specs=(vmem,) * 5,
        name="write_out",
    )(*outs)
    return (outs[0].reshape(shape),) + tuple(outs[1:])


def solution(mesh):
    sizes = tuple(mesh.shape[name] for name in AXES)
    grid = P("gx", "gy", "gz", None, None)
    return jax.shard_map(
        functools.partial(on_device, sizes),
        mesh=mesh,
        in_specs=(grid, grid, P("gz"), P(), P(), P(), P()),
        out_specs=(grid, P(), P(), P(), P()),
        check_vma=False,
    )
```
